32 devices in a mesh: fish: 2 (over y), img: 16 (over z, x, core).
Axes of the slice: x: 2, y: 2, z: 4, core: 2. Of those that a mesh axis runs over, the one named last changes fastest.
Arguments:
- img_feat: bfloat16 [64, 16384], P(None, ('fish', 'img')), parts along dimension 1, may hold values from -80 to 80
- mdl_feat: bfloat16 [64, 2048], P(None, ('fish', 'img')), parts along dimension 1, may hold values from -80 to 80
- img_mass: float32 [16384], P(('fish', 'img')), parts along dimension 0, may hold values from 0.5 to 2
- mdl_mass: float32 [2048], P('fish'), parts along dimension 0, may hold values from 0.5 to 2
Outputs:
- grad_img: float32 [64, 16384], P(None, ('fish', 'img')), parts along dimension 1
- grad_mdl: float32 [64, 2048], P(None, ('fish', 'img')), parts along dimension 1
The draws below stay inside these ranges and needn't reach their ends.
There are 2 independent parts, one for each index of `fish`. The reference program is written for one: setup_inputs(seed, part) draws one part's arguments, and reference() takes and returns one part's arrays. A program takes and returns all parts, laid end to end along the dimension named above; each array names one. Nothing has to cross between parts.
All inputs are finite; a program needn't handle non-finite values.
Results may differ from the reference program's by a relative error of at most 0.005.
Values may be sent and summed in bfloat16 or wider, within the bound.
No kernel may reach another device: no remote copies, remote signals or barrier semaphores. Data moves between devices by JAX's collectives and lax.ppermute only.
A program may use at most 64 MiB of HBM per device.

```python
import math
import jax
import jax.numpy as jnp
from jax import lax

FEAT = 64
ROWS_DEV = 512
ITERS = 4
IMAGED = 8192
MODEL = 1024


def paired_features(key):
    base_key, perm_key, noise_key, img_scale_key, mdl_scale_key = jax.random.split(jax.random.fold_in(key, 11), 5)
    base = jnp.clip(jax.random.normal(base_key, (FEAT, IMAGED), jnp.float32), -4.0, 4.0)
    noise = 0.8 * jnp.clip(jax.random.normal(noise_key, (FEAT, MODEL), jnp.float32), -4.0, 4.0)
    chosen = jax.random.permutation(perm_key, IMAGED)[:MODEL]
    matched = base[:, chosen] + noise
    img_scale = jnp.exp(jax.random.uniform(img_scale_key, (1, IMAGED), jnp.float32, 0.0, 2.3))
    mdl_scale = jnp.exp(jax.random.uniform(mdl_scale_key, (1, MODEL), jnp.float32, 0.0, 2.3))
    return (base * img_scale, matched * mdl_scale)


def draw_img_feat(key, part):
    return paired_features(key)[0].astype(jnp.bfloat16)


def draw_mdl_feat(key, part):
    return paired_features(key)[1].astype(jnp.bfloat16)


def steps_of(stream_key, extent, cuts, least, top_value):
    def one(position, parts):
        heights = jax.random.uniform(jax.random.fold_in(jax.random.fold_in(stream_key, 6), position), (parts,), jnp.float32, least / len(cuts), top_value / len(cuts))
        return jnp.repeat(jnp.exp(heights), extent[position] // parts).reshape((-1,) + (1,) * (len(extent) - position - 1))

    loudness = one(*cuts[0])
    for cut in cuts[1:]:
        loudness = loudness * one(*cut)
    return loudness


def setup_inputs(seed: int = 0, part: int = 0) -> dict:
    streams_of = jax.random.split(jax.random.key(seed), 5)
    part_splits = jax.random.split(jax.random.fold_in(streams_of[4], part), 5)
    img_feat = draw_img_feat(jax.random.fold_in(jax.random.fold_in(streams_of[4], part), 71), part)
    mdl_feat = draw_mdl_feat(jax.random.fold_in(jax.random.fold_in(streams_of[4], part), 71), part)
    img_mass = jnp.clip(jnp.exp(math.log(2.0) - 1.3862944 * jax.random.uniform(part_splits[2], (IMAGED,), jnp.float32) ** steps_of(part_splits[2], (IMAGED,), ((0, 16),), -0.2, 0.2)), 0.5, 2.0)
    mdl_mass = jnp.clip(jnp.exp(jax.random.uniform(part_splits[3], (MODEL,), jnp.float32, math.log(0.5), math.log(2.0))), 0.5, 2.0)
    return {"img_feat": img_feat, "mdl_feat": mdl_feat, "img_mass": img_mass, "mdl_mass": mdl_mass}


inv_temp = 20.0

def normalize(features):
    wide = features.astype(jnp.float32)
    guarded = lax.optimization_barrier(jnp.mean(wide * wide, axis=0, keepdims=True)) + 1e-06
    return (wide * lax.rsqrt(guarded)).astype(jnp.bfloat16)

def reference(img_feat, mdl_feat, img_mass, mdl_mass):
    factor = inv_temp / FEAT
    imaged_unit = normalize(img_feat)
    model_unit = normalize(mdl_feat)
    nblocks = IMAGED // ROWS_DEV
    model_wide = model_unit.astype(jnp.float32)
    row_blocks = imaged_unit.reshape(FEAT, nblocks, ROWS_DEV).transpose(1, 0, 2)

    def build(unit_block):
        scores = jnp.dot(unit_block.astype(jnp.float32).T, model_wide)
        return jnp.exp(scores * factor).astype(jnp.bfloat16)
    kernel = lax.map(build, row_blocks)
    col_scale = jnp.ones((MODEL,), jnp.float32)
    col_low = col_scale.astype(jnp.bfloat16)
    row_scale = jnp.ones((IMAGED,), jnp.float32)
    for iteration in range(ITERS):
        low_wide = col_low.astype(jnp.float32)
        row_sums = lax.map(lambda tile_block: jnp.dot(tile_block.astype(jnp.float32), low_wide), kernel)
        row_scale = img_mass / row_sums.reshape(IMAGED)
        row_low = row_scale.astype(jnp.bfloat16).astype(jnp.float32).reshape(nblocks, ROWS_DEV)

        def add_cols(carry, pair):
            tile_block, low_block = pair
            return (carry + jnp.dot(low_block, tile_block.astype(jnp.float32)), None)
        col_sum, unused = lax.scan(add_cols, jnp.zeros((MODEL,), jnp.float32), (kernel, row_low))
        col_scale = mdl_mass / col_sum
        col_low = col_scale.astype(jnp.bfloat16)
    weighted = (model_wide * col_scale[None, :]).astype(jnp.bfloat16).astype(jnp.float32)
    image_terms = lax.map(lambda tile_block: jnp.dot(weighted, tile_block.astype(jnp.float32).T), kernel)
    image_terms = image_terms.transpose(1, 0, 2).reshape(FEAT, IMAGED)
    grad_img = -(image_terms * row_scale[None, :])
    row_feat = (imaged_unit.astype(jnp.float32) * row_scale[None, :]).astype(jnp.bfloat16).astype(jnp.float32)
    feat_blocks = row_feat.reshape(FEAT, nblocks, ROWS_DEV).transpose(1, 0, 2)

    def add_model(carry, pair):
        tile_block, feat_block = pair
        return (carry + jnp.dot(tile_block.astype(jnp.float32).T, feat_block.T), None)
    model_terms, unused = lax.scan(add_model, jnp.zeros((MODEL, FEAT), jnp.float32), (kernel, feat_blocks))
    grad_mdl = -(model_terms.T * col_scale[None, :])
    return (grad_img, grad_mdl)
```

```python
import jax
import jax.numpy as jnp
from jax import lax
from jax.sharding import PartitionSpec as P

FEAT = 64
ITERS = 4


inv_temp = 20.0


def normalize(features):
    wide = features.astype(jnp.float32)
    guarded = jnp.mean(wide * wide, axis=0, keepdims=True) + 1e-06
    return (wide * lax.rsqrt(guarded)).astype(jnp.bfloat16)


def everyone(block, count):
    copies = jnp.broadcast_to(block, (count,) + block.shape)
    return lax.all_to_all(copies, "img", 0, 0)


def shards(count, img_feat, mdl_feat, img_mass, mdl_mass):
    factor = inv_temp / FEAT
    share = mdl_feat.shape[1]
    local_rows = img_feat.shape[1]
    imaged_unit = normalize(img_feat)
    blocks = everyone(normalize(mdl_feat), count)
    model_unit = blocks.transpose(1, 0, 2).reshape(FEAT, count * share)
    scores = lax.dot_general(
        imaged_unit, model_unit, (((0,), (0,)), ((), ())), preferred_element_type=jnp.float32
    )
    kernel = jnp.exp(scores * factor).astype(jnp.bfloat16)
    col_scale = jnp.ones((count * share,), jnp.float32)
    col_low = col_scale.astype(jnp.bfloat16)
    row_scale = jnp.ones((local_rows,), jnp.float32)
    for iteration in range(ITERS):
        row_scale = img_mass / jnp.dot(kernel, col_low, preferred_element_type=jnp.float32)
        partial_cols = jnp.dot(
            row_scale.astype(jnp.bfloat16), kernel, preferred_element_type=jnp.float32
        )
        col_scale = mdl_mass / jnp.sum(everyone(partial_cols, count), axis=0)
        col_low = col_scale.astype(jnp.bfloat16)
    weighted = (model_unit.astype(jnp.float32) * col_scale[None, :]).astype(jnp.bfloat16)
    grad_img = -(
        lax.dot_general(
            weighted, kernel, (((1,), (1,)), ((), ())), preferred_element_type=jnp.float32
        )
        * row_scale[None, :]
    )
    row_feat = (imaged_unit.astype(jnp.float32) * row_scale[None, :]).astype(jnp.bfloat16)
    terms = lax.dot_general(
        row_feat, kernel, (((1,), (0,)), ((), ())), preferred_element_type=jnp.float32
    )
    terms = terms.reshape(FEAT, count, share).transpose(1, 0, 2)
    summed = jnp.sum(lax.all_to_all(terms, "img", 0, 0), axis=0)
    offset = lax.axis_index("img") * share
    own_scale = lax.dynamic_slice_in_dim(col_scale, offset, share, 0)
    grad_mdl = -(summed * own_scale[None, :])
    return (grad_img, grad_mdl)


def solution(mesh):
    count = mesh.shape["img"]
    placed = (P(None, ("fish", "img")), P(None, ("fish", "img")), P(("fish", "img")), P("fish"))
    return jax.shard_map(
        lambda *args: shards(count, *args),
        mesh=mesh,
        in_specs=placed,
        out_specs=(P(None, ("fish", "img")), P(None, ("fish", "img"))),
        check_vma=False,
    )
```

```python
import functools
import jax
import jax.numpy as jnp
from jax import lax
from jax.experimental import pallas as pl
from jax.experimental.pallas import tpu as pltpu
from jax.sharding import PartitionSpec as P

FEAT = 64
ITERS = 4
LANES = 128
BF16 = jnp.bfloat16
F32 = jnp.float32

inv_temp = 20.0

RESIDENT = 24 << 20
GRANT = 12 << 20
WHOLE = pl.BlockSpec(memory_space=pltpu.VMEM)


def call(body, outs, *args):
    return pl.pallas_call(
        body,
        out_shape=outs,
        in_specs=[WHOLE] * len(args),
        out_specs=jax.tree.map(lambda _: WHOLE, outs),
        compiler_params=pltpu.CompilerParams(vmem_limit_bytes=GRANT),
    )(*args)


def shape(*dims, dtype=F32):
    return jax.ShapeDtypeStruct(dims, dtype)


def normalize(features):
    wide = features.astype(F32)
    guarded = jnp.mean(wide * wide, axis=0, keepdims=True) + 1e-06
    return (wide * lax.rsqrt(guarded)).astype(BF16)


def matmul(left, right):
    return lax.dot_general(left, right, (((1,), (0,)), ((), ())), preferred_element_type=F32)


def slots_of(groups):
    far = [s for s in range(2, groups, 2)]
    return [0, 1] + far + [s ^ 1 for s in far]


def pack(img_ref, mdl_ref, mass_ref, out_ref):
    rows = img_ref.shape[1]
    chunks = rows // LANES
    out_ref[:, :rows] = normalize(img_ref[...])
    unit = normalize(mdl_ref[...]).astype(F32)
    half = FEAT // 2
    share = unit.shape[1]
    out_ref[:half, rows : rows + share] = unit[:half].astype(BF16)
    out_ref[:half, rows + share :] = unit[half:].astype(BF16)
    mass = mass_ref[...]
    high = mass.astype(BF16)
    rest = mass - high.astype(F32)
    middle = rest.astype(BF16)
    low = (rest - middle.astype(F32)).astype(BF16)
    terms = [t.astype(F32) for t in (high, middle, low)]
    spare = half - 3 * chunks
    terms = jnp.concatenate(terms + [jnp.zeros((spare, LANES), F32)], axis=0)
    out_ref[half:, rows:] = terms.astype(BF16)


def collect(rows, own_ref, near_ref, far_ref, cross_ref, out_ref):
    half = FEAT // 2
    count = far_ref.shape[0] // FEAT
    places = [(own_ref, 0), (near_ref, 0)]
    places += [(far_ref, k) for k in range(count)] + [(cross_ref, k) for k in range(count)]
    for slot, (ref, k) in enumerate(places):
        out_ref[slot * half : (slot + 1) * half, :] = ref[k * FEAT : k * FEAT + half, rows:]


def build(
    groups,
    rows,
    own_ref,
    near_ref,
    far_ref,
    cross_ref,
    mine_ref,
    other_ref,
    mdl_mass_ref,
    kernel_ref,
    turned_ref,
    img_ref,
    mdl_ref,
    mass_ref,
    cols_mass_ref,
    sums_ref,
):
    half = FEAT // 2
    chunks = rows // LANES
    count = far_ref.shape[0] // FEAT
    place = lax.axis_index("img")
    group = place // 2
    first = place % 2 == 0
    places = [(own_ref, 0), (near_ref, 0)]
    places += [(far_ref, k) for k in range(count)] + [(cross_ref, k) for k in range(count)]
    low_lanes = lax.broadcasted_iota(jnp.int32, (FEAT, LANES), 1) < LANES // 2
    for slot, (distance, (ref, k)) in enumerate(zip(slots_of(groups), places)):
        part = ref.at[k * FEAT : (k + 1) * FEAT, :]
        img_ref[:, slot * rows : (slot + 1) * rows] = part[:, :rows]
        terms = part[half:, rows:].astype(F32)
        mass = terms[:chunks] + terms[chunks : 2 * chunks] + terms[2 * chunks : 3 * chunks]
        for j in range(chunks):
            at = slot * rows + j * LANES
            mass_ref[:, at : at + LANES] = mass[j : j + 1]
        sides = []
        for side in (mine_ref, other_ref):
            both = side[slot * half : (slot + 1) * half, :].astype(F32)
            sides.append(jnp.concatenate([both, pltpu.roll(both, LANES // 2, 1)], axis=0))
        left = jnp.where(first, sides[0], sides[1])
        right = jnp.where(first, sides[1], sides[0])
        pair = jnp.where(low_lanes, left, pltpu.roll(right, LANES // 2, 1))
        mdl_ref[:, slot * LANES : (slot + 1) * LANES] = pair.astype(BF16)
        cols_mass_ref[:, slot * LANES : (slot + 1) * LANES] = mdl_mass_ref[
            pl.ds(jnp.bitwise_xor(group, distance), 1), :
        ]

    models = mdl_ref.shape[1]
    sums_ref[...] = jnp.zeros_like(sums_ref)
    ones = jnp.ones((8, models), BF16)

    def block(index, carry):
        at = pl.ds(pl.multiple_of(index * rows, rows), rows)
        scores = lax.dot_general(
            img_ref[:, at], mdl_ref[...], (((0,), (0,)), ((), ())), preferred_element_type=F32
        )
        tile = jnp.exp(scores * (inv_temp / FEAT)).astype(BF16)
        kernel_ref[at, :] = tile
        turned_ref[:, at] = tile.T
        row_sums = matmul(ones, turned_ref[:, at])
        row_scale = mass_ref[:, at] / row_sums
        sums_ref[...] += matmul(row_scale.astype(BF16), kernel_ref[at, :])[:1]
        return carry

    lax.fori_loop(0, groups, block, 0)


def scaled(mine_ref, other_ref, cols_mass_ref):
    return cols_mass_ref[...] / (mine_ref[...] + other_ref[...])


def row_scales(col_scale, mass_ref, turned_ref):
    low = jnp.broadcast_to(col_scale.astype(BF16), (8, col_scale.shape[1]))
    return mass_ref[...] / matmul(low, turned_ref[...])


def iterate(mine_ref, other_ref, cols_mass_ref, mass_ref, kernel_ref, turned_ref, out_ref):
    col_scale = scaled(mine_ref, other_ref, cols_mass_ref)
    row_scale = row_scales(col_scale, mass_ref, turned_ref)
    out_ref[...] = matmul(row_scale.astype(BF16), kernel_ref[...])[:1]


def last(
    rows,
    mine_ref,
    other_ref,
    cols_mass_ref,
    mass_ref,
    kernel_ref,
    turned_ref,
    img_ref,
    out_ref,
    scale_ref,
):
    col_scale = scaled(mine_ref, other_ref, cols_mass_ref)
    row_scale = row_scales(col_scale, mass_ref, turned_ref)
    scale_ref[...] = row_scale[:1, :rows]
    sums = matmul(row_scale.astype(BF16), kernel_ref[...])[:1]
    tiles = sums.shape[1] // LANES
    for slot in range(tiles):
        out_ref[slot : slot + 1, :] = sums[:, slot * LANES : (slot + 1) * LANES]
    row_feat = (img_ref[...].astype(F32) * row_scale[:1]).astype(BF16)
    out_ref[tiles:, :] = matmul(row_feat, kernel_ref[:, :LANES])


def finish(
    mine_ref, other_ref, cols_mass_ref, scale_ref, mdl_ref, turned_ref, grad_img_ref, grad_mdl_ref
):
    rows = scale_ref.shape[1]
    tiles = mdl_ref.shape[1] // LANES
    total = mine_ref[:tiles, :] + other_ref[:tiles, :]
    col_scale = jnp.concatenate([total[k : k + 1] for k in range(tiles)], axis=1)
    col_scale = cols_mass_ref[...] / col_scale
    weighted = (mdl_ref[...].astype(F32) * col_scale).astype(BF16)
    grad_img_ref[...] = -(matmul(weighted, turned_ref[:, :rows]) * scale_ref[...])
    terms = mine_ref[tiles:, :] + other_ref[tiles:, :]
    terms = -(terms * col_scale[:, :LANES])
    first = lax.axis_index("img") % 2 == 0
    terms = jnp.where(first, terms, pltpu.roll(terms, LANES // 2, 1))
    grad_mdl_ref[...] = terms[:, : grad_mdl_ref.shape[1]]


def replicated(count, img_feat, mdl_feat, img_mass, mdl_mass):
    groups = count // 2
    rows, share = img_feat.shape[1], mdl_feat.shape[1]
    held, models = groups * rows, count * share

    def swap(block, distance):
        return lax.ppermute(block, "img", [(i, i ^ distance) for i in range(count)])

    packed = call(
        pack, shape(FEAT, rows + LANES, dtype=BF16), img_feat, mdl_feat, img_mass.reshape(-1, LANES)
    )
    far = jnp.concatenate([swap(packed, 2 * s) for s in range(2, groups, 2)], axis=0)
    near = swap(packed, 2)
    cross = swap(far, 2)
    pieces = (packed, near, far, cross)
    mine = call(
        functools.partial(collect, rows), shape(groups * FEAT // 2, LANES, dtype=BF16), *pieces
    )
    outs = (
        shape(held, models, dtype=BF16),
        shape(models, held, dtype=BF16),
        shape(FEAT, held, dtype=BF16),
        shape(FEAT, models, dtype=BF16),
        shape(1, held),
        shape(1, models),
        shape(1, models),
    )
    kernel, turned, img_unit, mdl_unit, mass, cols_mass, sums = call(
        functools.partial(build, groups, rows),
        outs,
        *pieces,
        mine,
        swap(mine, 1),
        mdl_mass.reshape(-1, LANES),
    )
    for iteration in range(1, ITERS - 1):
        sums = call(
            iterate, shape(1, models), sums, swap(sums, 1), cols_mass, mass, kernel, turned
        )
    both, row_scale = call(
        functools.partial(last, rows),
        (shape(models // LANES + FEAT, LANES), shape(1, rows)),
        sums,
        swap(sums, 1),
        cols_mass,
        mass,
        kernel,
        turned,
        img_unit,
    )
    return call(
        finish,
        (shape(FEAT, rows), shape(FEAT, share)),
        both,
        swap(both, 1),
        cols_mass,
        row_scale,
        mdl_unit,
        turned,
    )


def split(img_feat, mdl_feat, img_mass, mdl_mass):
    factor = inv_temp / FEAT
    share = mdl_feat.shape[1]
    img_unit = normalize(img_feat)
    mdl_unit = lax.all_gather(normalize(mdl_feat), "img", axis=1, tiled=True)
    scores = lax.dot_general(
        img_unit, mdl_unit, (((0,), (0,)), ((), ())), preferred_element_type=F32
    )
    kernel = jnp.exp(scores * factor).astype(BF16)
    col_low = jnp.ones((mdl_unit.shape[1],), BF16)
    for iteration in range(ITERS):
        row_scale = img_mass / jnp.dot(kernel, col_low, preferred_element_type=F32)
        sums = jnp.dot(row_scale.astype(BF16), kernel, preferred_element_type=F32)
        col_scale = mdl_mass / lax.psum(sums, "img")
        col_low = col_scale.astype(BF16)
    weighted = (mdl_unit.astype(F32) * col_scale[None, :]).astype(BF16)
    grad_img = lax.dot_general(
        weighted, kernel, (((1,), (1,)), ((), ())), preferred_element_type=F32
    )
    grad_img = -(grad_img * row_scale[None, :])
    row_feat = (img_unit.astype(F32) * row_scale[None, :]).astype(BF16)
    terms = lax.dot_general(
        kernel, row_feat, (((0,), (1,)), ((), ())), preferred_element_type=F32
    )
    summed = lax.psum_scatter(terms, "img", scatter_dimension=0, tiled=True)
    offset = lax.axis_index("img") * share
    own_scale = lax.dynamic_slice_in_dim(col_scale, offset, share, 0)
    grad_mdl = -(summed * own_scale[:, None]).T
    return (grad_img, grad_mdl)


def shards(count, img_feat, mdl_feat, img_mass, mdl_mass):
    groups = count // 2
    rows, share = img_feat.shape[1], mdl_feat.shape[1]
    resident = 2 * 2 * (groups * rows) * (count * share)
    fits = (
        count == 2 * groups
        and groups >= 4
        and groups & (groups - 1) == 0
        and 2 * share == LANES
        and rows % LANES == 0
        and 3 * (rows // LANES) <= FEAT // 2
        and resident <= RESIDENT
    )
    if fits:
        return replicated(count, img_feat, mdl_feat, img_mass, mdl_mass)
    return split(img_feat, mdl_feat, img_mass, mdl_mass)


def solution(mesh):
    placed = (P(None, ("fish", "img")), P(None, ("fish", "img")), P(("fish", "img")), P("fish"))
    return jax.shard_map(
        functools.partial(shards, mesh.shape["img"]),
        mesh=mesh,
        in_specs=placed,
        out_specs=(P(None, ("fish", "img")), P(None, ("fish", "img"))),
        check_vma=False,
    )
```

```python
import functools
import jax
import jax.numpy as jnp
from jax import lax
from jax.experimental import pallas as pl
from jax.experimental.pallas import tpu as pltpu
from jax.sharding import PartitionSpec as P

FEAT = 64
ITERS = 4
LANES = 128
BF16 = jnp.bfloat16
F32 = jnp.float32

inv_temp = 20.0

RESIDENT = 24 << 20
GRANT = 12 << 20
SIZE = 512
COST = 400
WHOLE = pl.BlockSpec(memory_space=pltpu.VMEM)


def call(body, outs, *args, alias=None, specs=None, scratch=(), flops=0):
    return pl.pallas_call(
        body,
        out_shape=outs,
        in_specs=specs or [WHOLE] * len(args),
        out_specs=jax.tree.map(lambda _: WHOLE, outs),
        scratch_shapes=scratch,
        input_output_aliases=alias or {},
        compiler_params=pltpu.CompilerParams(vmem_limit_bytes=GRANT),
        cost_estimate=pl.CostEstimate(flops=flops, bytes_accessed=flops // 512, transcendentals=0),
    )(*args)


def shape(*dims, dtype=F32):
    return jax.ShapeDtypeStruct(dims, dtype)


def normalize(features):
    wide = features.astype(F32)
    guarded = jnp.mean(wide * wide, axis=0, keepdims=True) + 1e-06
    return (wide * lax.rsqrt(guarded)).astype(BF16)


def matmul(left, right):
    return lax.dot_general(left, right, (((1,), (0,)), ((), ())), preferred_element_type=F32)


def fetch(img_hbm, mdl_hbm, mass_hbm, cols_hbm, out_ref, cols_ref, img_ref, mdl_ref, mass_ref, sems):
    pairs = ((img_hbm, img_ref), (mdl_hbm, mdl_ref), (mass_hbm, mass_ref), (cols_hbm, cols_ref))
    copies = [pltpu.make_async_copy(a, b, sems.at[k]) for k, (a, b) in enumerate(pairs)]
    for copy in copies:
        copy.start()
    for copy in copies:
        copy.wait()
    rows = img_ref.shape[1]
    chunks = rows // LANES
    out_ref[:, :rows] = normalize(img_ref[...])
    unit = normalize(mdl_ref[...]).astype(F32)
    half = FEAT // 2
    share = unit.shape[1]
    out_ref[:half, rows : rows + share] = unit[:half].astype(BF16)
    out_ref[:half, rows + share :] = unit[half:].astype(BF16)
    mass = mass_ref[...]
    high = mass.astype(BF16)
    rest = mass - high.astype(F32)
    middle = rest.astype(BF16)
    low = (rest - middle.astype(F32)).astype(BF16)
    terms = [t.astype(F32) for t in (high, middle, low)]
    spare = half - 3 * chunks
    terms = jnp.concatenate(terms + [jnp.zeros((spare, LANES), F32)], axis=0)
    out_ref[half:, rows:] = terms.astype(BF16)


def collect(rows, *refs):
    half = FEAT // 2
    out_ref = refs[-1]
    for slot, ref in enumerate(refs[:-1]):
        out_ref[slot * half : (slot + 1) * half, :] = ref[:half, rows:]


def gather_rows(refs, img_ref, mass_ref):
    half = FEAT // 2
    rows = img_ref.shape[1] // len(refs)
    chunks = rows // LANES
    for slot, ref in enumerate(refs):
        img_ref[:, slot * rows : (slot + 1) * rows] = ref[:, :rows]
        terms = ref[half:, rows:].astype(F32)
        mass = terms[:chunks] + terms[chunks : 2 * chunks] + terms[2 * chunks : 3 * chunks]
        for j in range(chunks):
            at = slot * rows + j * LANES
            mass_ref[:, at : at + LANES] = mass[j : j + 1]


def gather_models(distances, mine_ref, other_ref, mdl_mass_ref, mdl_ref, cols_mass_ref):
    half = FEAT // 2
    place = lax.axis_index("img")
    first = place % 2 == 0
    low_lanes = lax.broadcasted_iota(jnp.int32, (FEAT, LANES), 1) < LANES // 2
    for slot, distance in enumerate(distances):
        sides = []
        for side in (mine_ref, other_ref):
            both = side[slot * half : (slot + 1) * half, :].astype(F32)
            sides.append(jnp.concatenate([both, pltpu.roll(both, LANES // 2, 1)], axis=0))
        left = jnp.where(first, sides[0], sides[1])
        right = jnp.where(first, sides[1], sides[0])
        pair = jnp.where(low_lanes, left, pltpu.roll(right, LANES // 2, 1))
        mdl_ref[:, slot * LANES : (slot + 1) * LANES] = pair.astype(BF16)
        cols_mass_ref[:, slot * LANES : (slot + 1) * LANES] = mdl_mass_ref[
            pl.ds(jnp.bitwise_xor(place // 2, distance), 1), :
        ]


def fill(img_ref, row_at, mdl_ref, cols, kernel_ref, turned_ref, size, also=None):
    def block(index, carry):
        start = pl.multiple_of(index * size, size)
        scores = lax.dot_general(
            img_ref[:, pl.ds(start, size)],
            mdl_ref[...],
            (((0,), (0,)), ((), ())),
            preferred_element_type=F32,
        )
        tile = jnp.exp(scores * (inv_temp / FEAT)).astype(BF16)
        at = pl.ds(pl.multiple_of(row_at + start, size), size)
        kernel_ref[at, cols] = tile
        turned_ref[cols, at] = tile.T
        if also is not None:
            also(at)
        return carry

    lax.fori_loop(0, img_ref.shape[1] // size, block, 0)


def build_first(distances, *refs):
    pieces, refs = refs[: len(distances)], refs[len(distances) :]
    mine_ref, other_ref, mdl_mass_ref, kernel_ref, turned_ref = refs[:5]
    img_ref, mass_ref, mdl_ref, cols_mass_ref = refs[5:]
    gather_rows(pieces, img_ref, mass_ref)
    gather_models(distances, mine_ref, other_ref, mdl_mass_ref, mdl_ref, cols_mass_ref)
    cols = slice(0, mdl_ref.shape[1])
    fill(img_ref, 0, mdl_ref, cols, kernel_ref, turned_ref, SIZE)


def build_rows(count, *refs):
    pieces, refs = refs[:count], refs[count:]
    mdl_ref, _, _, kernel_ref, turned_ref, img_ref, mass_ref = refs
    gather_rows(pieces, img_ref, mass_ref)
    cols = slice(0, mdl_ref.shape[1])
    fill(img_ref, img_ref.shape[1], mdl_ref, cols, kernel_ref, turned_ref, SIZE)


def build_cols(
    distances,
    mine_ref,
    other_ref,
    mdl_mass_ref,
    img_even_ref,
    img_odd_ref,
    mass_even_ref,
    mass_odd_ref,
    _kernel,
    _turned,
    kernel_ref,
    turned_ref,
    mdl_ref,
    cols_mass_ref,
    sums_ref,
):
    gather_models(distances, mine_ref, other_ref, mdl_mass_ref, mdl_ref, cols_mass_ref)
    half = mdl_ref.shape[1]
    cols = slice(half, 2 * half)
    ones = jnp.ones((8, 2 * half), BF16)
    sums_ref[...] = jnp.zeros_like(sums_ref)

    for part, (img_ref, mass_ref) in enumerate(
        ((img_even_ref, mass_even_ref), (img_odd_ref, mass_odd_ref))
    ):
        base = part * img_ref.shape[1]

        def first_iteration(at, base=base, mass_ref=mass_ref):
            row_sums = matmul(ones, turned_ref[:, at])
            start = pl.multiple_of(at.start - base, at.size)
            row_scale = mass_ref[:, pl.ds(start, at.size)] / row_sums
            sums_ref[...] += matmul(row_scale.astype(BF16), kernel_ref[at, :])[:1]

        fill(img_ref, base, mdl_ref, cols, kernel_ref, turned_ref, SIZE, first_iteration)


def joined(refs):
    return jnp.concatenate([ref[...] for ref in refs], axis=1)


def scaled(mine_ref, other_ref, cols_mass):
    return joined(cols_mass) / (mine_ref[...] + other_ref[...])


def row_scales(col_scale, mass, turned_ref):
    low = jnp.broadcast_to(col_scale.astype(BF16), (8, col_scale.shape[1]))
    return joined(mass) / matmul(low, turned_ref[...])


def iterate(mine_ref, other_ref, ce_ref, co_ref, me_ref, mo_ref, kernel_ref, turned_ref, out_ref):
    col_scale = scaled(mine_ref, other_ref, (ce_ref, co_ref))
    row_scale = row_scales(col_scale, (me_ref, mo_ref), turned_ref)
    out_ref[...] = matmul(row_scale.astype(BF16), kernel_ref[...])[:1]


def last(
    rows,
    mine_ref,
    other_ref,
    ce_ref,
    co_ref,
    me_ref,
    mo_ref,
    kernel_ref,
    turned_ref,
    ie_ref,
    io_ref,
    out_ref,
    scale_ref,
):
    col_scale = scaled(mine_ref, other_ref, (ce_ref, co_ref))
    row_scale = row_scales(col_scale, (me_ref, mo_ref), turned_ref)
    scale_ref[...] = row_scale[:1, :rows]
    sums = matmul(row_scale.astype(BF16), kernel_ref[...])[:1]
    tiles = sums.shape[1] // LANES
    for slot in range(tiles):
        out_ref[slot : slot + 1, :] = sums[:, slot * LANES : (slot + 1) * LANES]
    row_feat = (joined((ie_ref, io_ref)).astype(F32) * row_scale[:1]).astype(BF16)
    out_ref[tiles:, :] = matmul(row_feat, kernel_ref[:, :LANES])


def finish(
    mine_ref,
    other_ref,
    ce_ref,
    co_ref,
    scale_ref,
    ue_ref,
    uo_ref,
    turned_ref,
    grad_img_ref,
    grad_mdl_ref,
):
    rows = scale_ref.shape[1]
    tiles = turned_ref.shape[0] // LANES
    total = mine_ref[:tiles, :] + other_ref[:tiles, :]
    col_sums = jnp.concatenate([total[k : k + 1] for k in range(tiles)], axis=1)
    col_scale = joined((ce_ref, co_ref)) / col_sums
    weighted = (joined((ue_ref, uo_ref)).astype(F32) * col_scale).astype(BF16)
    grad_img_ref[...] = -(matmul(weighted, turned_ref[:, :rows]) * scale_ref[...])
    terms = mine_ref[tiles:, :] + other_ref[tiles:, :]
    terms = -(terms * col_scale[:, :LANES])
    first = lax.axis_index("img") % 2 == 0
    terms = jnp.where(first, terms, pltpu.roll(terms, LANES // 2, 1))
    grad_mdl_ref[...] = terms[:, : grad_mdl_ref.shape[1]]


def replicated(count, img_feat, mdl_feat, img_mass, mdl_mass):
    groups = count // 2
    rows, share = img_feat.shape[1], mdl_feat.shape[1]
    held, models = groups * rows, count * share
    even = list(range(0, groups, 2))
    odd = [s + 1 for s in even]

    def swap(block, distance):
        return lax.ppermute(block, "img", [(i, i ^ distance) for i in range(count)])

    arguments = (img_feat, mdl_feat, img_mass.reshape(-1, LANES), mdl_mass.reshape(-1, LANES))
    packed, cols = call(
        fetch,
        (shape(FEAT, rows + LANES, dtype=BF16), shape(models // LANES, LANES)),
        *[pltpu.with_memory_space_constraint(x, pltpu.HBM) for x in arguments],
        specs=[pl.BlockSpec(memory_space=pltpu.HBM)] * 4,
        scratch=[
            pltpu.VMEM((FEAT, rows), BF16),
            pltpu.VMEM((FEAT, share), BF16),
            pltpu.VMEM((rows // LANES, LANES), F32),
            pltpu.SemaphoreType.DMA((4,)),
        ],
    )
    far = [swap(packed, 2 * s) for s in even[1:]]
    near = swap(packed, 2)
    along = [packed] + far
    across = [near] + [swap(block, 2) for block in far]

    def models_of(blocks):
        out = shape(len(blocks) * FEAT // 2, LANES, dtype=BF16)
        mine = call(functools.partial(collect, rows), out, *blocks)
        return mine, swap(mine, 1)

    halves = (shape(FEAT, held // 2, dtype=BF16), shape(1, held // 2))
    sides = (shape(FEAT, models // 2, dtype=BF16), shape(1, models // 2))
    whole = (shape(held, models, dtype=BF16), shape(models, held, dtype=BF16))
    kernel, turned, img_even, mass_even, mdl_even, cols_even = call(
        functools.partial(build_first, even), whole + halves + sides, *along, *models_of(along), cols,
        flops=held * models // 4 * COST,
    )
    kernel, turned, img_odd, mass_odd = call(
        functools.partial(build_rows, len(across)),
        whole + halves,
        *across,
        mdl_even,
        kernel,
        turned,
        alias={len(across) + 1: 0, len(across) + 2: 1},
        flops=held * models // 4 * COST,
    )
    kernel, turned, mdl_odd, cols_odd, sums = call(
        functools.partial(build_cols, odd),
        whole + sides + (shape(1, models),),
        *models_of(across),
        cols,
        img_even,
        img_odd,
        mass_even,
        mass_odd,
        kernel,
        turned,
        alias={7: 0, 8: 1},
        flops=held * models * COST,
    )
    fixed = (cols_even, cols_odd, mass_even, mass_odd, kernel, turned)
    for iteration in range(1, ITERS - 1):
        sums = call(iterate, shape(1, models), sums, swap(sums, 1), *fixed)
    both, row_scale = call(
        functools.partial(last, rows),
        (shape(models // LANES + FEAT, LANES), shape(1, rows)),
        sums,
        swap(sums, 1),
        *fixed,
        img_even,
        img_odd,
    )
    return call(
        finish,
        (shape(FEAT, rows), shape(FEAT, share)),
        both,
        swap(both, 1),
        cols_even,
        cols_odd,
        row_scale,
        mdl_even,
        mdl_odd,
        turned,
    )


def split(img_feat, mdl_feat, img_mass, mdl_mass):
    factor = inv_temp / FEAT
    share = mdl_feat.shape[1]
    img_unit = normalize(img_feat)
    mdl_unit = lax.all_gather(normalize(mdl_feat), "img", axis=1, tiled=True)
    scores = lax.dot_general(
        img_unit, mdl_unit, (((0,), (0,)), ((), ())), preferred_element_type=F32
    )
    kernel = jnp.exp(scores * factor).astype(BF16)
    col_low = jnp.ones((mdl_unit.shape[1],), BF16)
    for iteration in range(ITERS):
        row_scale = img_mass / jnp.dot(kernel, col_low, preferred_element_type=F32)
        sums = jnp.dot(row_scale.astype(BF16), kernel, preferred_element_type=F32)
        col_scale = mdl_mass / lax.psum(sums, "img")
        col_low = col_scale.astype(BF16)
    weighted = (mdl_unit.astype(F32) * col_scale[None, :]).astype(BF16)
    grad_img = lax.dot_general(
        weighted, kernel, (((1,), (1,)), ((), ())), preferred_element_type=F32
    )
    grad_img = -(grad_img * row_scale[None, :])
    row_feat = (img_unit.astype(F32) * row_scale[None, :]).astype(BF16)
    terms = lax.dot_general(
        kernel, row_feat, (((0,), (1,)), ((), ())), preferred_element_type=F32
    )
    summed = lax.psum_scatter(terms, "img", scatter_dimension=0, tiled=True)
    offset = lax.axis_index("img") * share
    own_scale = lax.dynamic_slice_in_dim(col_scale, offset, share, 0)
    grad_mdl = -(summed * own_scale[:, None]).T
    return (grad_img, grad_mdl)


def shards(count, img_feat, mdl_feat, img_mass, mdl_mass):
    groups = count // 2
    rows, share = img_feat.shape[1], mdl_feat.shape[1]
    resident = 2 * 2 * (groups * rows) * (count * share)
    fits = (
        count == 2 * groups
        and groups >= 4
        and groups & (groups - 1) == 0
        and 2 * share == LANES
        and rows % LANES == 0
        and 3 * (rows // LANES) <= FEAT // 2
        and resident <= RESIDENT
    )
    if fits:
        return replicated(count, img_feat, mdl_feat, img_mass, mdl_mass)
    return split(img_feat, mdl_feat, img_mass, mdl_mass)


def solution(mesh):
    placed = (P(None, ("fish", "img")), P(None, ("fish", "img")), P(("fish", "img")), P("fish"))
    return jax.shard_map(
        functools.partial(shards, mesh.shape["img"]),
        mesh=mesh,
        in_specs=placed,
        out_specs=(P(None, ("fish", "img")), P(None, ("fish", "img"))),
        check_vma=False,
    )
```

```python
import functools
import jax
import jax.numpy as jnp
from jax import lax
from jax.experimental import pallas as pl
from jax.experimental.pallas import tpu as pltpu
from jax.sharding import PartitionSpec as P

FEAT = 64
ITERS = 4
LANES = 128
BF16 = jnp.bfloat16
F32 = jnp.float32

inv_temp = 20.0

RESIDENT = 24 << 20
GRANT = 12 << 20
COST = 400
WHOLE = pl.BlockSpec(memory_space=pltpu.VMEM)


def call(body, outs, *args, alias=None, specs=None, scratch=(), flops=0):
    return pl.pallas_call(
        body,
        out_shape=outs,
        in_specs=specs or [WHOLE] * len(args),
        out_specs=jax.tree.map(lambda _: WHOLE, outs),
        scratch_shapes=scratch,
        input_output_aliases=alias or {},
        compiler_params=pltpu.CompilerParams(vmem_limit_bytes=GRANT),
        cost_estimate=pl.CostEstimate(flops=flops, bytes_accessed=flops // 512, transcendentals=0),
    )(*args)


def shape(*dims, dtype=F32):
    return jax.ShapeDtypeStruct(dims, dtype)


def normalize(features):
    wide = features.astype(F32)
    guarded = jnp.mean(wide * wide, axis=0, keepdims=True) + 1e-06
    return (wide * lax.rsqrt(guarded)).astype(BF16)


def matmul(left, right):
    return lax.dot_general(left, right, (((1,), (0,)), ((), ())), preferred_element_type=F32)


def fetch(img_hbm, mdl_hbm, mass_hbm, cols_hbm, out_ref, cols_ref, img_ref, mdl_ref, mass_ref, sems):
    pairs = ((img_hbm, img_ref), (mdl_hbm, mdl_ref), (mass_hbm, mass_ref), (cols_hbm, cols_ref))
    copies = [pltpu.make_async_copy(a, b, sems.at[k]) for k, (a, b) in enumerate(pairs)]
    for copy in copies:
        copy.start()
    for copy in copies:
        copy.wait()
    rows = img_ref.shape[1]
    chunks = rows // LANES
    out_ref[:, :rows] = normalize(img_ref[...])
    unit = normalize(mdl_ref[...]).astype(F32)
    half = FEAT // 2
    share = unit.shape[1]
    out_ref[:half, rows : rows + share] = unit[:half].astype(BF16)
    out_ref[:half, rows + share :] = unit[half:].astype(BF16)
    mass = mass_ref[...]
    high = mass.astype(BF16)
    rest = mass - high.astype(F32)
    middle = rest.astype(BF16)
    low = (rest - middle.astype(F32)).astype(BF16)
    terms = [t.astype(F32) for t in (high, middle, low)]
    spare = half - 3 * chunks
    terms = jnp.concatenate(terms + [jnp.zeros((spare, LANES), F32)], axis=0)
    out_ref[half:, rows:] = terms.astype(BF16)


def collect(rows, *refs):
    half = FEAT // 2
    out_ref = refs[-1]
    for slot, ref in enumerate(refs[:-1]):
        out_ref[slot * half : (slot + 1) * half, :] = ref[:half, rows:]


def gather_rows(refs, img_ref, mass_ref):
    half = FEAT // 2
    rows = img_ref.shape[1] // len(refs)
    chunks = rows // LANES
    for slot, ref in enumerate(refs):
        img_ref[:, slot * rows : (slot + 1) * rows] = ref[:, :rows]
        terms = ref[half:, rows:].astype(F32)
        mass = terms[:chunks] + terms[chunks : 2 * chunks] + terms[2 * chunks : 3 * chunks]
        for j in range(chunks):
            at = slot * rows + j * LANES
            mass_ref[:, at : at + LANES] = mass[j : j + 1]


def gather_models(distances, mine_ref, other_ref, mdl_mass_ref, mdl_ref, cols_mass_ref):
    half = FEAT // 2
    place = lax.axis_index("img")
    first = place % 2 == 0
    low_lanes = lax.broadcasted_iota(jnp.int32, (FEAT, LANES), 1) < LANES // 2
    for slot, distance in enumerate(distances):
        sides = []
        for side in (mine_ref, other_ref):
            both = side[slot * half : (slot + 1) * half, :].astype(F32)
            sides.append(jnp.concatenate([both, pltpu.roll(both, LANES // 2, 1)], axis=0))
        left = jnp.where(first, sides[0], sides[1])
        right = jnp.where(first, sides[1], sides[0])
        pair = jnp.where(low_lanes, left, pltpu.roll(right, LANES // 2, 1))
        mdl_ref[:, slot * LANES : (slot + 1) * LANES] = pair.astype(BF16)
        cols_mass_ref[:, slot * LANES : (slot + 1) * LANES] = mdl_mass_ref[
            pl.ds(jnp.bitwise_xor(place // 2, distance), 1), :
        ]


def fill(img_ref, rows, mdl_ref, cols, kernel_ref, turned_ref):
    scores = lax.dot_general(
        img_ref[...], mdl_ref[...], (((0,), (0,)), ((), ())), preferred_element_type=F32
    )
    tile = jnp.exp(scores * (inv_temp / FEAT)).astype(BF16)
    kernel_ref[rows, cols] = tile
    turned_ref[cols, rows] = tile.T


def halves_of(extent):
    return slice(0, extent // 2), slice(extent // 2, extent)


def build_first(distances, *refs):
    pieces, refs = refs[: len(distances)], refs[len(distances) :]
    mine_ref, other_ref, mdl_mass_ref, kernel_ref, turned_ref = refs[:5]
    img_ref, mass_ref, mdl_ref, cols_mass_ref = refs[5:]
    gather_rows(pieces, img_ref, mass_ref)
    gather_models(distances, mine_ref, other_ref, mdl_mass_ref, mdl_ref, cols_mass_ref)
    rows, cols = (halves_of(extent)[0] for extent in kernel_ref.shape)
    fill(img_ref, rows, mdl_ref, cols, kernel_ref, turned_ref)


def build_rows(count, *refs):
    pieces, refs = refs[:count], refs[count:]
    mdl_ref, _, _, kernel_ref, turned_ref, img_ref, mass_ref = refs
    gather_rows(pieces, img_ref, mass_ref)
    rows, cols = halves_of(kernel_ref.shape[0])[1], halves_of(kernel_ref.shape[1])[0]
    fill(img_ref, rows, mdl_ref, cols, kernel_ref, turned_ref)


def build_cols(
    distances,
    mine_ref,
    other_ref,
    mdl_mass_ref,
    img_even_ref,
    img_odd_ref,
    mass_even_ref,
    mass_odd_ref,
    _kernel,
    _turned,
    kernel_ref,
    turned_ref,
    mdl_ref,
    cols_mass_ref,
    sums_ref,
):
    gather_models(distances, mine_ref, other_ref, mdl_mass_ref, mdl_ref, cols_mass_ref)
    cols = halves_of(kernel_ref.shape[1])[1]
    for rows, img_ref in zip(halves_of(kernel_ref.shape[0]), (img_even_ref, img_odd_ref)):
        fill(img_ref, rows, mdl_ref, cols, kernel_ref, turned_ref)
    ones = jnp.ones((1, kernel_ref.shape[1]), F32)
    row_scale = row_scales(ones, (mass_even_ref, mass_odd_ref), turned_ref)
    sums_ref[...] = matmul(row_scale.astype(BF16), kernel_ref[...])[:1]


def joined(refs):
    return jnp.concatenate([ref[...] for ref in refs], axis=1)


def scaled(mine_ref, other_ref, cols_mass):
    return joined(cols_mass) / (mine_ref[...] + other_ref[...])


def row_scales(col_scale, mass, turned_ref):
    low = jnp.broadcast_to(col_scale.astype(BF16), (8, col_scale.shape[1]))
    return joined(mass) / matmul(low, turned_ref[...])


def iterate(mine_ref, other_ref, ce_ref, co_ref, me_ref, mo_ref, kernel_ref, turned_ref, out_ref):
    col_scale = scaled(mine_ref, other_ref, (ce_ref, co_ref))
    row_scale = row_scales(col_scale, (me_ref, mo_ref), turned_ref)
    out_ref[...] = matmul(row_scale.astype(BF16), kernel_ref[...])[:1]


def last(
    rows,
    mine_ref,
    other_ref,
    ce_ref,
    co_ref,
    me_ref,
    mo_ref,
    kernel_ref,
    turned_ref,
    ie_ref,
    io_ref,
    out_ref,
    scale_ref,
):
    col_scale = scaled(mine_ref, other_ref, (ce_ref, co_ref))
    row_scale = row_scales(col_scale, (me_ref, mo_ref), turned_ref)
    scale_ref[...] = row_scale[:1, :rows]
    sums = matmul(row_scale.astype(BF16), kernel_ref[...])[:1]
    tiles = sums.shape[1] // LANES
    for slot in range(tiles):
        out_ref[slot : slot + 1, :] = sums[:, slot * LANES : (slot + 1) * LANES]
    row_feat = (joined((ie_ref, io_ref)).astype(F32) * row_scale[:1]).astype(BF16)
    out_ref[tiles:, :] = matmul(row_feat, kernel_ref[:, :LANES])


def finish(
    mine_ref,
    other_ref,
    ce_ref,
    co_ref,
    scale_ref,
    ue_ref,
    uo_ref,
    turned_ref,
    grad_img_ref,
    grad_mdl_ref,
):
    rows = scale_ref.shape[1]
    tiles = turned_ref.shape[0] // LANES
    total = mine_ref[:tiles, :] + other_ref[:tiles, :]
    col_sums = jnp.concatenate([total[k : k + 1] for k in range(tiles)], axis=1)
    col_scale = joined((ce_ref, co_ref)) / col_sums
    weighted = (joined((ue_ref, uo_ref)).astype(F32) * col_scale).astype(BF16)
    grad_img_ref[...] = -(matmul(weighted, turned_ref[:, :rows]) * scale_ref[...])
    terms = mine_ref[tiles:, :] + other_ref[tiles:, :]
    terms = -(terms * col_scale[:, :LANES])
    first = lax.axis_index("img") % 2 == 0
    terms = jnp.where(first, terms, pltpu.roll(terms, LANES // 2, 1))
    grad_mdl_ref[...] = terms[:, : grad_mdl_ref.shape[1]]


def replicated(count, img_feat, mdl_feat, img_mass, mdl_mass):
    groups = count // 2
    rows, share = img_feat.shape[1], mdl_feat.shape[1]
    held, models = groups * rows, count * share
    even = list(range(0, groups, 2))
    odd = [s + 1 for s in even]

    def swap(block, distance):
        return lax.ppermute(block, "img", [(i, i ^ distance) for i in range(count)])

    arguments = (img_feat, mdl_feat, img_mass.reshape(-1, LANES), mdl_mass.reshape(-1, LANES))
    packed, cols = call(
        fetch,
        (shape(FEAT, rows + LANES, dtype=BF16), shape(models // LANES, LANES)),
        *[pltpu.with_memory_space_constraint(x, pltpu.HBM) for x in arguments],
        specs=[pl.BlockSpec(memory_space=pltpu.HBM)] * 4,
        scratch=[
            pltpu.VMEM((FEAT, rows), BF16),
            pltpu.VMEM((FEAT, share), BF16),
            pltpu.VMEM((rows // LANES, LANES), F32),
            pltpu.SemaphoreType.DMA((4,)),
        ],
    )
    far = [swap(packed, 2 * s) for s in even[1:]]
    near = swap(packed, 2)
    along = [packed] + far
    across = [near] + [swap(block, 2) for block in far]

    def models_of(blocks):
        out = shape(len(blocks) * FEAT // 2, LANES, dtype=BF16)
        mine = call(functools.partial(collect, rows), out, *blocks)
        return mine, swap(mine, 1)

    halves = (shape(FEAT, held // 2, dtype=BF16), shape(1, held // 2))
    sides = (shape(FEAT, models // 2, dtype=BF16), shape(1, models // 2))
    whole = (shape(held, models, dtype=BF16), shape(models, held, dtype=BF16))
    kernel, turned, img_even, mass_even, mdl_even, cols_even = call(
        functools.partial(build_first, even), whole + halves + sides, *along, *models_of(along), cols,
        flops=held * models // 4 * COST,
    )
    kernel, turned, img_odd, mass_odd = call(
        functools.partial(build_rows, len(across)),
        whole + halves,
        *across,
        mdl_even,
        kernel,
        turned,
        alias={len(across) + 1: 0, len(across) + 2: 1},
        flops=held * models // 4 * COST,
    )
    kernel, turned, mdl_odd, cols_odd, sums = call(
        functools.partial(build_cols, odd),
        whole + sides + (shape(1, models),),
        *models_of(across),
        cols,
        img_even,
        img_odd,
        mass_even,
        mass_odd,
        kernel,
        turned,
        alias={7: 0, 8: 1},
        flops=held * models * COST,
    )
    fixed = (cols_even, cols_odd, mass_even, mass_odd, kernel, turned)
    for iteration in range(1, ITERS - 1):
        sums = call(iterate, shape(1, models), sums, swap(sums, 1), *fixed)
    both, row_scale = call(
        functools.partial(last, rows),
        (shape(models // LANES + FEAT, LANES), shape(1, rows)),
        sums,
        swap(sums, 1),
        *fixed,
        img_even,
        img_odd,
    )
    return call(
        finish,
        (shape(FEAT, rows), shape(FEAT, share)),
        both,
        swap(both, 1),
        cols_even,
        cols_odd,
        row_scale,
        mdl_even,
        mdl_odd,
        turned,
    )


def split(img_feat, mdl_feat, img_mass, mdl_mass):
    factor = inv_temp / FEAT
    share = mdl_feat.shape[1]
    img_unit = normalize(img_feat)
    mdl_unit = lax.all_gather(normalize(mdl_feat), "img", axis=1, tiled=True)
    scores = lax.dot_general(
        img_unit, mdl_unit, (((0,), (0,)), ((), ())), preferred_element_type=F32
    )
    kernel = jnp.exp(scores * factor).astype(BF16)
    col_low = jnp.ones((mdl_unit.shape[1],), BF16)
    for iteration in range(ITERS):
        row_scale = img_mass / jnp.dot(kernel, col_low, preferred_element_type=F32)
        sums = jnp.dot(row_scale.astype(BF16), kernel, preferred_element_type=F32)
        col_scale = mdl_mass / lax.psum(sums, "img")
        col_low = col_scale.astype(BF16)
    weighted = (mdl_unit.astype(F32) * col_scale[None, :]).astype(BF16)
    grad_img = lax.dot_general(
        weighted, kernel, (((1,), (1,)), ((), ())), preferred_element_type=F32
    )
    grad_img = -(grad_img * row_scale[None, :])
    row_feat = (img_unit.astype(F32) * row_scale[None, :]).astype(BF16)
    terms = lax.dot_general(
        kernel, row_feat, (((0,), (1,)), ((), ())), preferred_element_type=F32
    )
    summed = lax.psum_scatter(terms, "img", scatter_dimension=0, tiled=True)
    offset = lax.axis_index("img") * share
    own_scale = lax.dynamic_slice_in_dim(col_scale, offset, share, 0)
    grad_mdl = -(summed * own_scale[:, None]).T
    return (grad_img, grad_mdl)


def shards(count, img_feat, mdl_feat, img_mass, mdl_mass):
    groups = count // 2
    rows, share = img_feat.shape[1], mdl_feat.shape[1]
    resident = 2 * 2 * (groups * rows) * (count * share)
    fits = (
        count == 2 * groups
        and groups >= 4
        and groups & (groups - 1) == 0
        and 2 * share == LANES
        and rows % LANES == 0
        and 3 * (rows // LANES) <= FEAT // 2
        and resident <= RESIDENT
    )
    if fits:
        return replicated(count, img_feat, mdl_feat, img_mass, mdl_mass)
    return split(img_feat, mdl_feat, img_mass, mdl_mass)


def solution(mesh):
    placed = (P(None, ("fish", "img")), P(None, ("fish", "img")), P(("fish", "img")), P("fish"))
    return jax.shard_map(
        functools.partial(shards, mesh.shape["img"]),
        mesh=mesh,
        in_specs=placed,
        out_specs=(P(None, ("fish", "img")), P(None, ("fish", "img"))),
        check_vma=False,
    )
```

```python
import functools
import jax
import jax.numpy as jnp
from jax import lax
from jax.experimental import pallas as pl
from jax.experimental.pallas import tpu as pltpu
from jax.sharding import PartitionSpec as P

FEAT = 64
ITERS = 4
LANES = 128
BF16 = jnp.bfloat16
F32 = jnp.float32

inv_temp = 20.0

RESIDENT = 24 << 20
GRANT = 12 << 20
COST = 400
WHOLE = pl.BlockSpec(memory_space=pltpu.VMEM)


def call(body, outs, *args, alias=None, specs=None, scratch=(), flops=0):
    return pl.pallas_call(
        body,
        out_shape=outs,
        in_specs=specs or [WHOLE] * len(args),
        out_specs=jax.tree.map(lambda _: WHOLE, outs),
        scratch_shapes=scratch,
        input_output_aliases=alias or {},
        compiler_params=pltpu.CompilerParams(vmem_limit_bytes=GRANT),
        cost_estimate=pl.CostEstimate(flops=flops, bytes_accessed=flops // 512, transcendentals=0),
    )(*args)


def shape(*dims, dtype=F32):
    return jax.ShapeDtypeStruct(dims, dtype)


def normalize(features):
    wide = features.astype(F32)
    guarded = jnp.mean(wide * wide, axis=0, keepdims=True) + 1e-06
    return (wide * lax.rsqrt(guarded)).astype(BF16)


def matmul(left, right):
    return lax.dot_general(left, right, (((1,), (0,)), ((), ())), preferred_element_type=F32)


def fetch(img_hbm, mdl_hbm, mass_hbm, cols_hbm, out_ref, cols_ref, img_ref, mdl_ref, mass_ref, sems):
    pairs = ((img_hbm, img_ref), (mdl_hbm, mdl_ref), (mass_hbm, mass_ref), (cols_hbm, cols_ref))
    copies = [pltpu.make_async_copy(a, b, sems.at[k]) for k, (a, b) in enumerate(pairs)]
    for copy in copies:
        copy.start()
    for copy in copies:
        copy.wait()
    rows = img_ref.shape[1]
    chunks = rows // LANES
    out_ref[:, :rows] = normalize(img_ref[...])
    unit = normalize(mdl_ref[...]).astype(F32)
    half = FEAT // 2
    share = unit.shape[1]
    out_ref[:half, rows : rows + share] = unit[:half].astype(BF16)
    out_ref[:half, rows + share :] = unit[half:].astype(BF16)
    mass = mass_ref[...]
    high = mass.astype(BF16)
    rest = mass - high.astype(F32)
    middle = rest.astype(BF16)
    low = (rest - middle.astype(F32)).astype(BF16)
    terms = [t.astype(F32) for t in (high, middle, low)]
    spare = half - 3 * chunks
    terms = jnp.concatenate(terms + [jnp.zeros((spare, LANES), F32)], axis=0)
    out_ref[half:, rows:] = terms.astype(BF16)


def collect(rows, *refs):
    half = FEAT // 2
    out_ref = refs[-1]
    for slot, ref in enumerate(refs[:-1]):
        out_ref[slot * half : (slot + 1) * half, :] = ref[:half, rows:]


def gather_rows(refs, img_ref, mass_ref):
    half = FEAT // 2
    rows = img_ref.shape[1] // len(refs)
    chunks = rows // LANES
    for slot, ref in enumerate(refs):
        img_ref[:, slot * rows : (slot + 1) * rows] = ref[:, :rows]
        terms = ref[half:, rows:].astype(F32)
        mass = terms[:chunks] + terms[chunks : 2 * chunks] + terms[2 * chunks : 3 * chunks]
        for j in range(chunks):
            at = slot * rows + j * LANES
            mass_ref[:, at : at + LANES] = mass[j : j + 1]


def gather_models(distances, mine_ref, other_ref, mdl_mass_ref, mdl_ref, cols_mass_ref):
    half = FEAT // 2
    place = lax.axis_index("img")
    first = place % 2 == 0
    low_lanes = lax.broadcasted_iota(jnp.int32, (FEAT, LANES), 1) < LANES // 2
    for slot, distance in enumerate(distances):
        sides = []
        for side in (mine_ref, other_ref):
            both = side[slot * half : (slot + 1) * half, :].astype(F32)
            sides.append(jnp.concatenate([both, pltpu.roll(both, LANES // 2, 1)], axis=0))
        left = jnp.where(first, sides[0], sides[1])
        right = jnp.where(first, sides[1], sides[0])
        pair = jnp.where(low_lanes, left, pltpu.roll(right, LANES // 2, 1))
        mdl_ref[:, slot * LANES : (slot + 1) * LANES] = pair.astype(BF16)
        cols_mass_ref[:, slot * LANES : (slot + 1) * LANES] = mdl_mass_ref[
            pl.ds(jnp.bitwise_xor(place // 2, distance), 1), :
        ]


def fill(img_ref, rows, mdl_ref, cols, kernel_ref, turned_ref):
    scores = lax.dot_general(
        img_ref[...], mdl_ref[...], (((0,), (0,)), ((), ())), preferred_element_type=F32
    )
    tile = jnp.exp(scores * (inv_temp / FEAT)).astype(BF16)
    kernel_ref[rows, cols] = tile
    turned_ref[cols, rows] = tile.T


def halves_of(extent):
    return slice(0, extent // 2), slice(extent // 2, extent)


def build_first(distances, *refs):
    pieces, refs = refs[: len(distances)], refs[len(distances) :]
    mine_ref, other_ref, mdl_mass_ref, kernel_ref, turned_ref = refs[:5]
    img_ref, mass_ref, mdl_ref, cols_mass_ref = refs[5:]
    gather_rows(pieces, img_ref, mass_ref)
    gather_models(distances, mine_ref, other_ref, mdl_mass_ref, mdl_ref, cols_mass_ref)
    rows, cols = (halves_of(extent)[0] for extent in kernel_ref.shape)
    fill(img_ref, rows, mdl_ref, cols, kernel_ref, turned_ref)


def build_rows(count, *refs):
    pieces, refs = refs[:count], refs[count:]
    mdl_ref, _, _, kernel_ref, turned_ref, img_ref, mass_ref = refs
    gather_rows(pieces, img_ref, mass_ref)
    rows, cols = halves_of(kernel_ref.shape[0])[1], halves_of(kernel_ref.shape[1])[0]
    fill(img_ref, rows, mdl_ref, cols, kernel_ref, turned_ref)


def build_cols(
    distances,
    mine_ref,
    other_ref,
    mdl_mass_ref,
    img_even_ref,
    img_odd_ref,
    mass_even_ref,
    mass_odd_ref,
    _kernel,
    _turned,
    kernel_ref,
    turned_ref,
    mdl_ref,
    cols_mass_ref,
    sums_ref,
):
    gather_models(distances, mine_ref, other_ref, mdl_mass_ref, mdl_ref, cols_mass_ref)
    cols = halves_of(kernel_ref.shape[1])[1]
    for rows, img_ref in zip(halves_of(kernel_ref.shape[0]), (img_even_ref, img_odd_ref)):
        fill(img_ref, rows, mdl_ref, cols, kernel_ref, turned_ref)
    ones = jnp.ones((1, kernel_ref.shape[1]), F32)
    row_scale = row_scales(ones, (mass_even_ref, mass_odd_ref), turned_ref)
    sums_ref[...] = matmul(row_scale.astype(BF16), kernel_ref[...])[:1]


def joined(refs):
    return jnp.concatenate([ref[...] for ref in refs], axis=1)


def scaled(mine_ref, other_ref, cols_mass):
    return joined(cols_mass) / (mine_ref[...] + other_ref[...])


def row_scales(col_scale, mass, turned_ref):
    low = jnp.broadcast_to(col_scale.astype(BF16), (8, col_scale.shape[1]))
    return joined(mass) / matmul(low, turned_ref[...])


def iterate(mine_ref, other_ref, ce_ref, co_ref, me_ref, mo_ref, kernel_ref, turned_ref, out_ref):
    col_scale = scaled(mine_ref, other_ref, (ce_ref, co_ref))
    row_scale = row_scales(col_scale, (me_ref, mo_ref), turned_ref)
    out_ref[...] = matmul(row_scale.astype(BF16), kernel_ref[...])[:1]


def last(
    rows,
    mine_ref,
    other_ref,
    ce_ref,
    co_ref,
    me_ref,
    mo_ref,
    kernel_ref,
    turned_ref,
    ie_ref,
    io_ref,
    out_ref,
    scale_ref,
):
    col_scale = scaled(mine_ref, other_ref, (ce_ref, co_ref))
    row_scale = row_scales(col_scale, (me_ref, mo_ref), turned_ref)
    scale_ref[...] = row_scale[:1, :rows]
    sums = matmul(row_scale.astype(BF16), kernel_ref[...])[:1]
    tiles = sums.shape[1] // LANES
    for slot in range(tiles):
        out_ref[slot : slot + 1, :] = sums[:, slot * LANES : (slot + 1) * LANES]
    row_feat = (joined((ie_ref, io_ref)).astype(F32) * row_scale[:1]).astype(BF16)
    out_ref[tiles:, :] = matmul(row_feat, kernel_ref[:, :LANES])


def finish(
    mine_ref,
    other_ref,
    ce_ref,
    co_ref,
    scale_ref,
    ue_ref,
    uo_ref,
    turned_ref,
    grad_img_ref,
    grad_mdl_ref,
):
    rows = scale_ref.shape[1]
    tiles = turned_ref.shape[0] // LANES
    total = mine_ref[:tiles, :] + other_ref[:tiles, :]
    col_sums = jnp.concatenate([total[k : k + 1] for k in range(tiles)], axis=1)
    col_scale = joined((ce_ref, co_ref)) / col_sums
    weighted = (joined((ue_ref, uo_ref)).astype(F32) * col_scale).astype(BF16)
    grad_img_ref[...] = -(matmul(weighted, turned_ref[:, :rows]) * scale_ref[...])
    terms = mine_ref[tiles:, :] + other_ref[tiles:, :]
    terms = -(terms * col_scale[:, :LANES])
    first = lax.axis_index("img") % 2 == 0
    terms = jnp.where(first, terms, pltpu.roll(terms, LANES // 2, 1))
    grad_mdl_ref[...] = terms[:, : grad_mdl_ref.shape[1]]


def replicated(count, img_feat, mdl_feat, img_mass, mdl_mass):
    groups = count // 2
    rows, share = img_feat.shape[1], mdl_feat.shape[1]
    held, models = groups * rows, count * share
    middle = groups // 2
    even = [0, middle] + [s for s in range(2, groups, 2) if s != middle]
    odd = [s + 1 for s in even]

    def swap(block, distance):
        return lax.ppermute(block, "img", [(i, i ^ distance) for i in range(count)])

    arguments = (img_feat, mdl_feat, img_mass.reshape(-1, LANES), mdl_mass.reshape(-1, LANES))
    packed, cols = call(
        fetch,
        (shape(FEAT, rows + LANES, dtype=BF16), shape(models // LANES, LANES)),
        *[pltpu.with_memory_space_constraint(x, pltpu.HBM) for x in arguments],
        specs=[pl.BlockSpec(memory_space=pltpu.HBM)] * 4,
        scratch=[
            pltpu.VMEM((FEAT, rows), BF16),
            pltpu.VMEM((FEAT, share), BF16),
            pltpu.VMEM((rows // LANES, LANES), F32),
            pltpu.SemaphoreType.DMA((4,)),
        ],
    )
    far = [swap(packed, 2 * s) for s in even[1:]]
    near = swap(packed, 2)
    along = [packed] + far
    across = [near] + [swap(block, 2) for block in far]

    def models_of(blocks):
        out = shape(len(blocks) * FEAT // 2, LANES, dtype=BF16)
        mine = call(functools.partial(collect, rows), out, *blocks)
        return mine, swap(mine, 1)

    halves = (shape(FEAT, held // 2, dtype=BF16), shape(1, held // 2))
    sides = (shape(FEAT, models // 2, dtype=BF16), shape(1, models // 2))
    whole = (shape(held, models, dtype=BF16), shape(models, held, dtype=BF16))
    kernel, turned, img_even, mass_even, mdl_even, cols_even = call(
        functools.partial(build_first, even), whole + halves + sides, *along, *models_of(along), cols,
        flops=held * models // 4 * COST,
    )
    kernel, turned, img_odd, mass_odd = call(
        functools.partial(build_rows, len(across)),
        whole + halves,
        *across,
        mdl_even,
        kernel,
        turned,
        alias={len(across) + 1: 0, len(across) + 2: 1},
        flops=held * models // 4 * COST,
    )
    kernel, turned, mdl_odd, cols_odd, sums = call(
        functools.partial(build_cols, odd),
        whole + sides + (shape(1, models),),
        *models_of(across),
        cols,
        img_even,
        img_odd,
        mass_even,
        mass_odd,
        kernel,
        turned,
        alias={7: 0, 8: 1},
        flops=held * models * COST,
    )
    fixed = (cols_even, cols_odd, mass_even, mass_odd, kernel, turned)
    for iteration in range(1, ITERS - 1):
        sums = call(iterate, shape(1, models), sums, swap(sums, 1), *fixed)
    both, row_scale = call(
        functools.partial(last, rows),
        (shape(models // LANES + FEAT, LANES), shape(1, rows)),
        sums,
        swap(sums, 1),
        *fixed,
        img_even,
        img_odd,
    )
    return call(
        finish,
        (shape(FEAT, rows), shape(FEAT, share)),
        both,
        swap(both, 1),
        cols_even,
        cols_odd,
        row_scale,
        mdl_even,
        mdl_odd,
        turned,
    )


def split(img_feat, mdl_feat, img_mass, mdl_mass):
    factor = inv_temp / FEAT
    share = mdl_feat.shape[1]
    img_unit = normalize(img_feat)
    mdl_unit = lax.all_gather(normalize(mdl_feat), "img", axis=1, tiled=True)
    scores = lax.dot_general(
        img_unit, mdl_unit, (((0,), (0,)), ((), ())), preferred_element_type=F32
    )
    kernel = jnp.exp(scores * factor).astype(BF16)
    col_low = jnp.ones((mdl_unit.shape[1],), BF16)
    for iteration in range(ITERS):
        row_scale = img_mass / jnp.dot(kernel, col_low, preferred_element_type=F32)
        sums = jnp.dot(row_scale.astype(BF16), kernel, preferred_element_type=F32)
        col_scale = mdl_mass / lax.psum(sums, "img")
        col_low = col_scale.astype(BF16)
    weighted = (mdl_unit.astype(F32) * col_scale[None, :]).astype(BF16)
    grad_img = lax.dot_general(
        weighted, kernel, (((1,), (1,)), ((), ())), preferred_element_type=F32
    )
    grad_img = -(grad_img * row_scale[None, :])
    row_feat = (img_unit.astype(F32) * row_scale[None, :]).astype(BF16)
    terms = lax.dot_general(
        kernel, row_feat, (((0,), (1,)), ((), ())), preferred_element_type=F32
    )
    summed = lax.psum_scatter(terms, "img", scatter_dimension=0, tiled=True)
    offset = lax.axis_index("img") * share
    own_scale = lax.dynamic_slice_in_dim(col_scale, offset, share, 0)
    grad_mdl = -(summed * own_scale[:, None]).T
    return (grad_img, grad_mdl)


def shards(count, img_feat, mdl_feat, img_mass, mdl_mass):
    groups = count // 2
    rows, share = img_feat.shape[1], mdl_feat.shape[1]
    resident = 2 * 2 * (groups * rows) * (count * share)
    fits = (
        count == 2 * groups
        and groups >= 4
        and groups & (groups - 1) == 0
        and 2 * share == LANES
        and rows % LANES == 0
        and 3 * (rows // LANES) <= FEAT // 2
        and resident <= RESIDENT
    )
    if fits:
        return replicated(count, img_feat, mdl_feat, img_mass, mdl_mass)
    return split(img_feat, mdl_feat, img_mass, mdl_mass)


def solution(mesh):
    placed = (P(None, ("fish", "img")), P(None, ("fish", "img")), P(("fish", "img")), P("fish"))
    return jax.shard_map(
        functools.partial(shards, mesh.shape["img"]),
        mesh=mesh,
        in_specs=placed,
        out_specs=(P(None, ("fish", "img")), P(None, ("fish", "img"))),
        check_vma=False,
    )
```

```python
import functools
import jax
import jax.numpy as jnp
from jax import lax
from jax.experimental import pallas as pl
from jax.experimental.pallas import tpu as pltpu
from jax.sharding import PartitionSpec as P

FEAT = 64
ITERS = 4
LANES = 128
BF16 = jnp.bfloat16
F32 = jnp.float32

inv_temp = 20.0

RESIDENT = 24 << 20
GRANT = 12 << 20
COST = 400
WHOLE = pl.BlockSpec(memory_space=pltpu.VMEM)


def call(body, outs, *args, alias=None, specs=None, scratch=(), flops=0):
    return pl.pallas_call(
        body,
        out_shape=outs,
        in_specs=specs or [WHOLE] * len(args),
        out_specs=jax.tree.map(lambda _: WHOLE, outs),
        scratch_shapes=scratch,
        input_output_aliases=alias or {},
        compiler_params=pltpu.CompilerParams(vmem_limit_bytes=GRANT),
        cost_estimate=pl.CostEstimate(flops=flops, bytes_accessed=flops // 512, transcendentals=0),
    )(*args)


def shape(*dims, dtype=F32):
    return jax.ShapeDtypeStruct(dims, dtype)


def normalize(features):
    wide = features.astype(F32)
    guarded = jnp.mean(wide * wide, axis=0, keepdims=True) + 1e-06
    return (wide * lax.rsqrt(guarded)).astype(BF16)


def matmul(left, right):
    return lax.dot_general(left, right, (((1,), (0,)), ((), ())), preferred_element_type=F32)


def fetch(img_hbm, mdl_hbm, mass_hbm, cols_hbm, out_ref, cols_ref, img_ref, mdl_ref, mass_ref, sems):
    pairs = ((img_hbm, img_ref), (mdl_hbm, mdl_ref), (mass_hbm, mass_ref), (cols_hbm, cols_ref))
    copies = [pltpu.make_async_copy(a, b, sems.at[k]) for k, (a, b) in enumerate(pairs)]
    for copy in copies:
        copy.start()
    for copy in copies:
        copy.wait()
    rows = img_ref.shape[1]
    chunks = rows // LANES
    out_ref[:, :rows] = normalize(img_ref[...])
    unit = normalize(mdl_ref[...]).astype(F32)
    half = FEAT // 2
    share = unit.shape[1]
    out_ref[:half, rows : rows + share] = unit[:half].astype(BF16)
    out_ref[:half, rows + share :] = unit[half:].astype(BF16)
    mass = mass_ref[...]
    high = mass.astype(BF16)
    rest = mass - high.astype(F32)
    middle = rest.astype(BF16)
    low = (rest - middle.astype(F32)).astype(BF16)
    terms = [t.astype(F32) for t in (high, middle, low)]
    spare = half - 3 * chunks
    terms = jnp.concatenate(terms + [jnp.zeros((spare, LANES), F32)], axis=0)
    out_ref[half:, rows:] = terms.astype(BF16)


def collect(rows, *refs):
    half = FEAT // 2
    out_ref = refs[-1]
    for slot, ref in enumerate(refs[:-1]):
        out_ref[slot * half : (slot + 1) * half, :] = ref[:half, rows:]


def gather_rows(refs, img_ref, mass_ref):
    half = FEAT // 2
    rows = img_ref.shape[1] // len(refs)
    chunks = rows // LANES
    for slot, ref in enumerate(refs):
        img_ref[:, slot * rows : (slot + 1) * rows] = ref[:, :rows]
        terms = ref[half:, rows:].astype(F32)
        mass = terms[:chunks] + terms[chunks : 2 * chunks] + terms[2 * chunks : 3 * chunks]
        for j in range(chunks):
            at = slot * rows + j * LANES
            mass_ref[:, at : at + LANES] = jnp.broadcast_to(mass[j : j + 1], (8, LANES))


def gather_models(distances, mine_ref, other_ref, mdl_mass_ref, mdl_ref, cols_mass_ref):
    half = FEAT // 2
    place = lax.axis_index("img")
    first = place % 2 == 0
    low_lanes = lax.broadcasted_iota(jnp.int32, (FEAT, LANES), 1) < LANES // 2
    for slot, distance in enumerate(distances):
        sides = []
        for side in (mine_ref, other_ref):
            both = side[slot * half : (slot + 1) * half, :].astype(F32)
            sides.append(jnp.concatenate([both, pltpu.roll(both, LANES // 2, 1)], axis=0))
        left = jnp.where(first, sides[0], sides[1])
        right = jnp.where(first, sides[1], sides[0])
        pair = jnp.where(low_lanes, left, pltpu.roll(right, LANES // 2, 1))
        mdl_ref[:, slot * LANES : (slot + 1) * LANES] = pair.astype(BF16)
        cols_mass_ref[:, slot * LANES : (slot + 1) * LANES] = mdl_mass_ref[
            pl.ds(jnp.bitwise_xor(place // 2, distance), 1), :
        ]


def fill(img_ref, rows, mdl_ref, cols, kernel_ref, turned_ref):
    scores = lax.dot_general(
        img_ref[...], mdl_ref[...], (((0,), (0,)), ((), ())), preferred_element_type=F32
    )
    tile = jnp.exp(scores * (inv_temp / FEAT)).astype(BF16)
    kernel_ref[rows, cols] = tile
    turned_ref[cols, rows] = tile.T


def fill_wide(img_ref, rows, mdl_ref, cols, kernel_ref, turned_ref, wide_ref):
    scores = lax.dot_general(
        mdl_ref[...], img_ref[...], (((0,), (0,)), ((), ())), preferred_element_type=F32
    )
    tile = jnp.exp(scores * (inv_temp / FEAT)).astype(BF16)
    turned_ref[cols, rows] = tile
    kernel_ref[rows, cols] = tile.T
    wide = tile.astype(F32)
    wide_ref[cols, :] = wide
    return jnp.sum(wide, axis=0, keepdims=True)


def halves_of(extent):
    return slice(0, extent // 2), slice(extent // 2, extent)


def build_first(distances, *refs):
    pieces, refs = refs[: len(distances)], refs[len(distances) :]
    mine_ref, other_ref, mdl_mass_ref, kernel_ref, turned_ref, wide_ref, known_ref = refs[:7]
    img_ref, mass_ref, mdl_ref, cols_mass_ref = refs[7:]
    gather_rows(pieces, img_ref, mass_ref)
    gather_models(distances, mine_ref, other_ref, mdl_mass_ref, mdl_ref, cols_mass_ref)
    rows, cols = (halves_of(extent)[0] for extent in kernel_ref.shape)
    known_ref[...] = fill_wide(img_ref, rows, mdl_ref, cols, kernel_ref, turned_ref, wide_ref)


def build_rows(count, *refs):
    pieces, refs = refs[:count], refs[count:]
    mdl_ref, _, _, kernel_ref, turned_ref, img_ref, mass_ref = refs
    gather_rows(pieces, img_ref, mass_ref)
    rows, cols = halves_of(kernel_ref.shape[0])[1], halves_of(kernel_ref.shape[1])[0]
    fill(img_ref, rows, mdl_ref, cols, kernel_ref, turned_ref)


def build_cols(
    distances,
    mine_ref,
    other_ref,
    mdl_mass_ref,
    img_even_ref,
    img_odd_ref,
    mass_even_ref,
    mass_odd_ref,
    known_ref,
    _kernel,
    _turned,
    _wide,
    kernel_ref,
    turned_ref,
    wide_ref,
    mdl_ref,
    cols_mass_ref,
    sums_ref,
    lanes_ref,
):
    gather_models(distances, mine_ref, other_ref, mdl_mass_ref, mdl_ref, cols_mass_ref)
    even, odd = halves_of(kernel_ref.shape[0])
    cols = halves_of(kernel_ref.shape[1])[1]
    fill(img_odd_ref, odd, mdl_ref, cols, kernel_ref, turned_ref)
    rest = fill_wide(img_even_ref, even, mdl_ref, cols, kernel_ref, turned_ref, wide_ref)
    row_scale = mass_even_ref[...] / (known_ref[...] + rest)
    ones = jnp.ones((8, kernel_ref.shape[1]), BF16)
    scales = (
        lambda: row_scale,
        lambda: mass_odd_ref[...] / matmul(ones, turned_ref[:, odd]),
    )
    sums_ref[...] = column_sums(scales, kernel_ref, wide_ref, lanes_ref)


def joined(refs):
    return jnp.concatenate([ref[...] for ref in refs], axis=1)


def scaled(mine_ref, other_ref, cols_mass):
    return joined(cols_mass) / (mine_ref[...] + other_ref[...])


def row_scales(col_scale, mass, turned_ref):
    low = jnp.broadcast_to(col_scale.astype(BF16), (8, col_scale.shape[1]))

    def of(mass_ref, rows):
        return lambda: mass_ref[...] / matmul(low, turned_ref[:, rows])

    return [of(*pair) for pair in zip(mass, halves_of(turned_ref.shape[1]))]


def column_sums(scales, kernel_ref, wide_ref, lanes_ref):
    even, odd = scales
    scale = even().astype(BF16).astype(F32)
    for at in range(0, wide_ref.shape[0], 8):
        part = None
        for lane in range(0, wide_ref.shape[1], LANES):
            lanes = slice(lane, lane + LANES)
            term = wide_ref[at : at + 8, lanes] * scale[:, lanes]
            part = term if part is None else part + term
        lanes_ref[at : at + 8, :] = part
    sums = matmul(odd().astype(BF16), kernel_ref[halves_of(kernel_ref.shape[0])[1], :])
    lanes = lanes_ref[...]
    high = lanes.astype(BF16)
    rest = (lanes - high.astype(F32)).astype(BF16)
    ones = jnp.ones((8, LANES), BF16)
    for part in (high, rest):
        sums += lax.dot_general(
            ones, part, (((1,), (1,)), ((), ())), preferred_element_type=F32
        )
    return sums[:1]


def iterate(
    mine_ref,
    other_ref,
    ce_ref,
    co_ref,
    me_ref,
    mo_ref,
    kernel_ref,
    turned_ref,
    wide_ref,
    out_ref,
    lanes_ref,
):
    col_scale = scaled(mine_ref, other_ref, (ce_ref, co_ref))
    scales = row_scales(col_scale, (me_ref, mo_ref), turned_ref)
    out_ref[...] = column_sums(scales, kernel_ref, wide_ref, lanes_ref)


def last(
    rows,
    mine_ref,
    other_ref,
    ce_ref,
    co_ref,
    me_ref,
    mo_ref,
    kernel_ref,
    turned_ref,
    wide_ref,
    ie_ref,
    io_ref,
    out_ref,
    scale_ref,
    lanes_ref,
):
    col_scale = scaled(mine_ref, other_ref, (ce_ref, co_ref))
    found = []

    def kept(scale):
        def of():
            found.append(scale())
            return found[-1]

        return of

    scales = [kept(scale) for scale in row_scales(col_scale, (me_ref, mo_ref), turned_ref)]
    sums = column_sums(scales, kernel_ref, wide_ref, lanes_ref)
    scale_ref[...] = found[0][:1, :rows]
    tiles = sums.shape[1] // LANES
    for slot in range(tiles):
        out_ref[slot : slot + 1, :] = sums[:, slot * LANES : (slot + 1) * LANES]
    terms = None
    for img_ref, scale, at in zip((ie_ref, io_ref), found, halves_of(kernel_ref.shape[0])):
        row_feat = (img_ref[...].astype(F32) * scale[:1]).astype(BF16)
        term = matmul(row_feat, kernel_ref[at, :LANES])
        terms = term if terms is None else terms + term
    out_ref[tiles:, :] = terms


def finish(
    mine_ref,
    other_ref,
    ce_ref,
    co_ref,
    scale_ref,
    ue_ref,
    uo_ref,
    turned_ref,
    grad_img_ref,
    grad_mdl_ref,
):
    rows = scale_ref.shape[1]
    tiles = turned_ref.shape[0] // LANES
    total = mine_ref[:tiles, :] + other_ref[:tiles, :]
    col_sums = jnp.concatenate([total[k : k + 1] for k in range(tiles)], axis=1)
    col_scale = joined((ce_ref, co_ref)) / col_sums
    weighted = (joined((ue_ref, uo_ref)).astype(F32) * col_scale).astype(BF16)
    grad_img_ref[...] = -(matmul(weighted, turned_ref[:, :rows]) * scale_ref[...])
    terms = mine_ref[tiles:, :] + other_ref[tiles:, :]
    terms = -(terms * col_scale[:, :LANES])
    first = lax.axis_index("img") % 2 == 0
    terms = jnp.where(first, terms, pltpu.roll(terms, LANES // 2, 1))
    grad_mdl_ref[...] = terms[:, : grad_mdl_ref.shape[1]]


def replicated(count, img_feat, mdl_feat, img_mass, mdl_mass):
    groups = count // 2
    rows, share = img_feat.shape[1], mdl_feat.shape[1]
    held, models = groups * rows, count * share
    middle = groups // 2
    even = [0] + [s for s in range(groups - 2, 0, -2) if s != middle] + [middle]
    odd = [s + 1 for s in even]

    def swap(block, distance):
        return lax.ppermute(block, "img", [(i, i ^ distance) for i in range(count)])

    arguments = (img_feat, mdl_feat, img_mass.reshape(-1, LANES), mdl_mass.reshape(-1, LANES))
    packed, cols = call(
        fetch,
        (shape(FEAT, rows + LANES, dtype=BF16), shape(models // LANES, LANES)),
        *[pltpu.with_memory_space_constraint(x, pltpu.HBM) for x in arguments],
        specs=[pl.BlockSpec(memory_space=pltpu.HBM)] * 4,
        scratch=[
            pltpu.VMEM((FEAT, rows), BF16),
            pltpu.VMEM((FEAT, share), BF16),
            pltpu.VMEM((rows // LANES, LANES), F32),
            pltpu.SemaphoreType.DMA((4,)),
        ],
    )
    far = [swap(packed, 2 * s) for s in even[1:]]
    near = swap(packed, 2)
    along = [packed] + far
    across = [near] + [swap(block, 2) for block in far]

    def models_of(blocks):
        out = shape(len(blocks) * FEAT // 2, LANES, dtype=BF16)
        mine = call(functools.partial(collect, rows), out, *blocks)
        return mine, swap(mine, 1)

    halves = (shape(FEAT, held // 2, dtype=BF16), shape(8, held // 2))
    sides = (shape(FEAT, models // 2, dtype=BF16), shape(1, models // 2))
    whole = (shape(held, models, dtype=BF16), shape(models, held, dtype=BF16))
    extra = (shape(models, held // 2),)
    lanes = [pltpu.VMEM((models, LANES), F32)]
    kernel, turned, wide, known, img_even, mass_even, mdl_even, cols_even = call(
        functools.partial(build_first, even),
        whole + extra + (shape(1, held // 2),) + halves + sides,
        *along, *models_of(along), cols,
        flops=held * models // 4 * COST,
    )
    kernel, turned, img_odd, mass_odd = call(
        functools.partial(build_rows, len(across)),
        whole + halves,
        *across,
        mdl_even,
        kernel,
        turned,
        alias={len(across) + 1: 0, len(across) + 2: 1},
        flops=held * models // 4 * COST,
    )
    kernel, turned, wide, mdl_odd, cols_odd, sums = call(
        functools.partial(build_cols, odd),
        whole + extra + sides + (shape(1, models),),
        *models_of(across),
        cols,
        img_even,
        img_odd,
        mass_even,
        mass_odd,
        known,
        kernel,
        turned,
        wide,
        alias={8: 0, 9: 1, 10: 2},
        scratch=lanes,
        flops=held * models * COST,
    )
    fixed = (cols_even, cols_odd, mass_even, mass_odd, kernel, turned, wide)
    for iteration in range(1, ITERS - 1):
        sums = call(iterate, shape(1, models), sums, swap(sums, 1), *fixed, scratch=lanes)
    both, row_scale = call(
        functools.partial(last, rows),
        (shape(models // LANES + FEAT, LANES), shape(1, rows)),
        sums,
        swap(sums, 1),
        *fixed,
        img_even,
        img_odd,
        scratch=lanes,
    )
    return call(
        finish,
        (shape(FEAT, rows), shape(FEAT, share)),
        both,
        swap(both, 1),
        cols_even,
        cols_odd,
        row_scale,
        mdl_even,
        mdl_odd,
        turned,
    )


def split(img_feat, mdl_feat, img_mass, mdl_mass):
    factor = inv_temp / FEAT
    share = mdl_feat.shape[1]
    img_unit = normalize(img_feat)
    mdl_unit = lax.all_gather(normalize(mdl_feat), "img", axis=1, tiled=True)
    scores = lax.dot_general(
        img_unit, mdl_unit, (((0,), (0,)), ((), ())), preferred_element_type=F32
    )
    kernel = jnp.exp(scores * factor).astype(BF16)
    col_low = jnp.ones((mdl_unit.shape[1],), BF16)
    for iteration in range(ITERS):
        row_scale = img_mass / jnp.dot(kernel, col_low, preferred_element_type=F32)
        sums = jnp.dot(row_scale.astype(BF16), kernel, preferred_element_type=F32)
        col_scale = mdl_mass / lax.psum(sums, "img")
        col_low = col_scale.astype(BF16)
    weighted = (mdl_unit.astype(F32) * col_scale[None, :]).astype(BF16)
    grad_img = lax.dot_general(
        weighted, kernel, (((1,), (1,)), ((), ())), preferred_element_type=F32
    )
    grad_img = -(grad_img * row_scale[None, :])
    row_feat = (img_unit.astype(F32) * row_scale[None, :]).astype(BF16)
    terms = lax.dot_general(
        kernel, row_feat, (((0,), (1,)), ((), ())), preferred_element_type=F32
    )
    summed = lax.psum_scatter(terms, "img", scatter_dimension=0, tiled=True)
    offset = lax.axis_index("img") * share
    own_scale = lax.dynamic_slice_in_dim(col_scale, offset, share, 0)
    grad_mdl = -(summed * own_scale[:, None]).T
    return (grad_img, grad_mdl)


def shards(count, img_feat, mdl_feat, img_mass, mdl_mass):
    groups = count // 2
    rows, share = img_feat.shape[1], mdl_feat.shape[1]
    resident = (2 + 2 + 4 // 2) * (groups * rows) * (count * share)
    fits = (
        count == 2 * groups
        and groups >= 4
        and groups & (groups - 1) == 0
        and 2 * share == LANES
        and rows % LANES == 0
        and 3 * (rows // LANES) <= FEAT // 2
        and resident <= RESIDENT
    )
    if fits:
        return replicated(count, img_feat, mdl_feat, img_mass, mdl_mass)
    return split(img_feat, mdl_feat, img_mass, mdl_mass)


def solution(mesh):
    placed = (P(None, ("fish", "img")), P(None, ("fish", "img")), P(("fish", "img")), P("fish"))
    return jax.shard_map(
        functools.partial(shards, mesh.shape["img"]),
        mesh=mesh,
        in_specs=placed,
        out_specs=(P(None, ("fish", "img")), P(None, ("fish", "img"))),
        check_vma=False,
    )
```

```python
import functools
import jax
import jax.numpy as jnp
from jax import lax
from jax.experimental import pallas as pl
from jax.experimental.pallas import tpu as pltpu
from jax.sharding import PartitionSpec as P

FEAT = 64
LOG2E = 1.4426950408889634
ITERS = 4
LANES = 128
BF16 = jnp.bfloat16
F32 = jnp.float32

inv_temp = 20.0

RESIDENT = 24 << 20
GRANT = 12 << 20
COST = 400
WHOLE = pl.BlockSpec(memory_space=pltpu.VMEM)


def call(body, outs, *args, alias=None, specs=None, scratch=(), flops=0):
    return pl.pallas_call(
        body,
        out_shape=outs,
        in_specs=specs or [WHOLE] * len(args),
        out_specs=jax.tree.map(lambda _: WHOLE, outs),
        scratch_shapes=scratch,
        input_output_aliases=alias or {},
        compiler_params=pltpu.CompilerParams(vmem_limit_bytes=GRANT),
        cost_estimate=pl.CostEstimate(flops=flops, bytes_accessed=flops // 512, transcendentals=0),
    )(*args)


def shape(*dims, dtype=F32):
    return jax.ShapeDtypeStruct(dims, dtype)


def normalize(features):
    wide = features.astype(F32)
    guarded = jnp.mean(wide * wide, axis=0, keepdims=True) + 1e-06
    return (wide * lax.rsqrt(guarded)).astype(BF16)


def matmul(left, right):
    return lax.dot_general(left, right, (((1,), (0,)), ((), ())), preferred_element_type=F32)


def fetch(img_hbm, mdl_hbm, mass_hbm, cols_hbm, out_ref, cols_ref, img_ref, mdl_ref, mass_ref, sems):
    pairs = ((img_hbm, img_ref), (mdl_hbm, mdl_ref), (mass_hbm, mass_ref), (cols_hbm, cols_ref))
    copies = [pltpu.make_async_copy(a, b, sems.at[k]) for k, (a, b) in enumerate(pairs)]
    for copy in copies:
        copy.start()
    for copy in copies:
        copy.wait()
    rows = img_ref.shape[1]
    chunks = rows // LANES
    out_ref[:, :rows] = normalize(img_ref[...])
    unit = normalize(mdl_ref[...]).astype(F32)
    half = FEAT // 2
    share = unit.shape[1]
    out_ref[:half, rows : rows + share] = unit[:half].astype(BF16)
    out_ref[:half, rows + share :] = unit[half:].astype(BF16)
    mass = mass_ref[...]
    high = mass.astype(BF16)
    rest = mass - high.astype(F32)
    middle = rest.astype(BF16)
    low = (rest - middle.astype(F32)).astype(BF16)
    terms = [t.astype(F32) for t in (high, middle, low)]
    spare = half - 3 * chunks
    terms = jnp.concatenate(terms + [jnp.zeros((spare, LANES), F32)], axis=0)
    out_ref[half:, rows:] = terms.astype(BF16)


def collect(rows, *refs):
    half = FEAT // 2
    out_ref = refs[-1]
    for slot, ref in enumerate(refs[:-1]):
        out_ref[slot * half : (slot + 1) * half, :] = ref[:half, rows:]


def gather_rows(refs, img_ref, mass_ref):
    half = FEAT // 2
    rows = img_ref.shape[1] // len(refs)
    chunks = rows // LANES
    for slot, ref in enumerate(refs):
        img_ref[:, slot * rows : (slot + 1) * rows] = ref[:, :rows]
        terms = ref[half:, rows:].astype(F32)
        mass = terms[:chunks] + terms[chunks : 2 * chunks] + terms[2 * chunks : 3 * chunks]
        for j in range(chunks):
            at = slot * rows + j * LANES
            mass_ref[:, at : at + LANES] = jnp.broadcast_to(mass[j : j + 1], (8, LANES))


def gather_models(distances, mine_ref, other_ref, mdl_mass_ref, mdl_ref, cols_mass_ref):
    half = FEAT // 2
    place = lax.axis_index("img")
    first = place % 2 == 0
    low_lanes = lax.broadcasted_iota(jnp.int32, (FEAT, LANES), 1) < LANES // 2
    for slot, distance in enumerate(distances):
        sides = []
        for side in (mine_ref, other_ref):
            both = side[slot * half : (slot + 1) * half, :].astype(F32)
            sides.append(jnp.concatenate([both, pltpu.roll(both, LANES // 2, 1)], axis=0))
        left = jnp.where(first, sides[0], sides[1])
        right = jnp.where(first, sides[1], sides[0])
        pair = jnp.where(low_lanes, left, pltpu.roll(right, LANES // 2, 1))
        mdl_ref[:, slot * LANES : (slot + 1) * LANES] = pair.astype(BF16)
        cols_mass_ref[:, slot * LANES : (slot + 1) * LANES] = mdl_mass_ref[
            pl.ds(jnp.bitwise_xor(place // 2, distance), 1), :
        ]


def fill(img_ref, rows, mdl_ref, cols, kernel_ref, turned_ref):
    scores = lax.dot_general(
        img_ref[...], mdl_ref[...], (((0,), (0,)), ((), ())), preferred_element_type=F32
    )
    tile = jnp.exp2(scores * (inv_temp / FEAT * LOG2E)).astype(BF16)
    kernel_ref[rows, cols] = tile
    turned_ref[cols, rows] = tile.T


def fill_wide(img_ref, rows, mdl_ref, cols, kernel_ref, turned_ref, wide_ref):
    scores = lax.dot_general(
        mdl_ref[...], img_ref[...], (((0,), (0,)), ((), ())), preferred_element_type=F32
    )
    tile = jnp.exp2(scores * (inv_temp / FEAT * LOG2E)).astype(BF16)
    turned_ref[cols, rows] = tile
    kernel_ref[rows, cols] = tile.T
    wide = tile.astype(F32)
    wide_ref[cols, :] = wide
    return jnp.sum(wide, axis=0, keepdims=True)


def halves_of(extent):
    return slice(0, extent // 2), slice(extent // 2, extent)


def build_first(distances, *refs):
    pieces, refs = refs[: len(distances)], refs[len(distances) :]
    mine_ref, other_ref, mdl_mass_ref, kernel_ref, turned_ref, wide_ref, known_ref = refs[:7]
    img_ref, mass_ref, mdl_ref, cols_mass_ref = refs[7:]
    gather_rows(pieces, img_ref, mass_ref)
    gather_models(distances, mine_ref, other_ref, mdl_mass_ref, mdl_ref, cols_mass_ref)
    rows, cols = (halves_of(extent)[0] for extent in kernel_ref.shape)
    known_ref[...] = fill_wide(img_ref, rows, mdl_ref, cols, kernel_ref, turned_ref, wide_ref)


def build_rows(count, *refs):
    pieces, refs = refs[:count], refs[count:]
    mdl_ref, _, _, kernel_ref, turned_ref, img_ref, mass_ref = refs
    gather_rows(pieces, img_ref, mass_ref)
    rows, cols = halves_of(kernel_ref.shape[0])[1], halves_of(kernel_ref.shape[1])[0]
    fill(img_ref, rows, mdl_ref, cols, kernel_ref, turned_ref)


def build_cols(
    distances,
    mine_ref,
    other_ref,
    mdl_mass_ref,
    img_even_ref,
    img_odd_ref,
    mass_even_ref,
    mass_odd_ref,
    known_ref,
    _kernel,
    _turned,
    _wide,
    kernel_ref,
    turned_ref,
    wide_ref,
    mdl_ref,
    cols_mass_ref,
    sums_ref,
    lanes_ref,
):
    gather_models(distances, mine_ref, other_ref, mdl_mass_ref, mdl_ref, cols_mass_ref)
    even, odd = halves_of(kernel_ref.shape[0])
    cols = halves_of(kernel_ref.shape[1])[1]
    fill(img_odd_ref, odd, mdl_ref, cols, kernel_ref, turned_ref)
    rest = fill_wide(img_even_ref, even, mdl_ref, cols, kernel_ref, turned_ref, wide_ref)
    row_scale = mass_even_ref[...] / (known_ref[...] + rest)
    ones = jnp.ones((8, kernel_ref.shape[1]), BF16)
    scales = (
        lambda: row_scale,
        lambda: mass_odd_ref[...] / matmul(ones, turned_ref[:, odd]),
    )
    sums_ref[...] = column_sums(scales, kernel_ref, wide_ref, lanes_ref)


def joined(refs):
    return jnp.concatenate([ref[...] for ref in refs], axis=1)


def scaled(mine_ref, other_ref, cols_mass):
    return joined(cols_mass) / (mine_ref[...] + other_ref[...])


def row_scales(col_scale, mass, turned_ref):
    low = jnp.broadcast_to(col_scale.astype(BF16), (8, col_scale.shape[1]))

    def of(mass_ref, rows):
        return lambda: mass_ref[...] / matmul(low, turned_ref[:, rows])

    return [of(*pair) for pair in zip(mass, halves_of(turned_ref.shape[1]))]


def column_sums(scales, kernel_ref, wide_ref, lanes_ref):
    even, odd = scales
    scale = even().astype(BF16).astype(F32)
    for at in range(0, wide_ref.shape[0], 8):
        part = None
        for lane in range(0, wide_ref.shape[1], LANES):
            lanes = slice(lane, lane + LANES)
            term = wide_ref[at : at + 8, lanes] * scale[:, lanes]
            part = term if part is None else part + term
        lanes_ref[at : at + 8, :] = part
    sums = matmul(odd().astype(BF16), kernel_ref[halves_of(kernel_ref.shape[0])[1], :])
    lanes = lanes_ref[...]
    high = lanes.astype(BF16)
    rest = (lanes - high.astype(F32)).astype(BF16)
    both = jnp.concatenate([high, rest], axis=1)
    ones = jnp.ones((8, 2 * LANES), BF16)
    sums += lax.dot_general(ones, both, (((1,), (1,)), ((), ())), preferred_element_type=F32)
    return sums[:1]


def iterate(
    mine_ref,
    other_ref,
    ce_ref,
    co_ref,
    me_ref,
    mo_ref,
    kernel_ref,
    turned_ref,
    wide_ref,
    out_ref,
    lanes_ref,
):
    col_scale = scaled(mine_ref, other_ref, (ce_ref, co_ref))
    scales = row_scales(col_scale, (me_ref, mo_ref), turned_ref)
    out_ref[...] = column_sums(scales, kernel_ref, wide_ref, lanes_ref)


def last(
    rows,
    mine_ref,
    other_ref,
    ce_ref,
    co_ref,
    me_ref,
    mo_ref,
    kernel_ref,
    turned_ref,
    wide_ref,
    ie_ref,
    io_ref,
    out_ref,
    scale_ref,
    lanes_ref,
):
    col_scale = scaled(mine_ref, other_ref, (ce_ref, co_ref))
    found = []

    def kept(scale):
        def of():
            found.append(scale())
            return found[-1]

        return of

    scales = [kept(scale) for scale in row_scales(col_scale, (me_ref, mo_ref), turned_ref)]
    sums = column_sums(scales, kernel_ref, wide_ref, lanes_ref)
    scale_ref[...] = found[0][:1, :rows]
    tiles = sums.shape[1] // LANES
    for slot in range(tiles):
        out_ref[slot : slot + 1, :] = sums[:, slot * LANES : (slot + 1) * LANES]
    terms = None
    for img_ref, scale, at in zip((ie_ref, io_ref), found, halves_of(kernel_ref.shape[0])):
        row_feat = (img_ref[...].astype(F32) * scale[:1]).astype(BF16)
        term = matmul(row_feat, kernel_ref[at, :LANES])
        terms = term if terms is None else terms + term
    out_ref[tiles:, :] = terms


def finish(
    mine_ref,
    other_ref,
    ce_ref,
    co_ref,
    scale_ref,
    ue_ref,
    uo_ref,
    turned_ref,
    grad_img_ref,
    grad_mdl_ref,
):
    rows = scale_ref.shape[1]
    tiles = turned_ref.shape[0] // LANES
    total = mine_ref[:tiles, :] + other_ref[:tiles, :]
    col_sums = jnp.concatenate([total[k : k + 1] for k in range(tiles)], axis=1)
    col_scale = joined((ce_ref, co_ref)) / col_sums
    weighted = (joined((ue_ref, uo_ref)).astype(F32) * col_scale).astype(BF16)
    grad_img_ref[...] = -(matmul(weighted, turned_ref[:, :rows]) * scale_ref[...])
    terms = mine_ref[tiles:, :] + other_ref[tiles:, :]
    terms = -(terms * col_scale[:, :LANES])
    first = lax.axis_index("img") % 2 == 0
    terms = jnp.where(first, terms, pltpu.roll(terms, LANES // 2, 1))
    grad_mdl_ref[...] = terms[:, : grad_mdl_ref.shape[1]]


def replicated(count, img_feat, mdl_feat, img_mass, mdl_mass):
    groups = count // 2
    rows, share = img_feat.shape[1], mdl_feat.shape[1]
    held, models = groups * rows, count * share
    middle = groups // 2
    even = [0] + [s for s in range(groups - 2, 0, -2) if s != middle] + [middle]
    odd = [s + 1 for s in even]

    def swap(block, distance):
        return lax.ppermute(block, "img", [(i, i ^ distance) for i in range(count)])

    arguments = (img_feat, mdl_feat, img_mass.reshape(-1, LANES), mdl_mass.reshape(-1, LANES))
    packed, cols = call(
        fetch,
        (shape(FEAT, rows + LANES, dtype=BF16), shape(models // LANES, LANES)),
        *[pltpu.with_memory_space_constraint(x, pltpu.HBM) for x in arguments],
        specs=[pl.BlockSpec(memory_space=pltpu.HBM)] * 4,
        scratch=[
            pltpu.VMEM((FEAT, rows), BF16),
            pltpu.VMEM((FEAT, share), BF16),
            pltpu.VMEM((rows // LANES, LANES), F32),
            pltpu.SemaphoreType.DMA((4,)),
        ],
    )
    far = [swap(packed, 2 * s) for s in even[1:]]
    near = swap(packed, 2)
    along = [packed] + far
    across = [near] + [swap(block, 2) for block in far]

    def models_of(blocks):
        out = shape(len(blocks) * FEAT // 2, LANES, dtype=BF16)
        mine = call(functools.partial(collect, rows), out, *blocks)
        return mine, swap(mine, 1)

    halves = (shape(FEAT, held // 2, dtype=BF16), shape(8, held // 2))
    sides = (shape(FEAT, models // 2, dtype=BF16), shape(1, models // 2))
    whole = (shape(held, models, dtype=BF16), shape(models, held, dtype=BF16))
    extra = (shape(models, held // 2),)
    lanes = [pltpu.VMEM((models, LANES), F32)]
    kernel, turned, wide, known, img_even, mass_even, mdl_even, cols_even = call(
        functools.partial(build_first, even),
        whole + extra + (shape(1, held // 2),) + halves + sides,
        *along, *models_of(along), cols,
        flops=held * models // 4 * COST,
    )
    kernel, turned, img_odd, mass_odd = call(
        functools.partial(build_rows, len(across)),
        whole + halves,
        *across,
        mdl_even,
        kernel,
        turned,
        alias={len(across) + 1: 0, len(across) + 2: 1},
        flops=held * models // 4 * COST,
    )
    kernel, turned, wide, mdl_odd, cols_odd, sums = call(
        functools.partial(build_cols, odd),
        whole + extra + sides + (shape(1, models),),
        *models_of(across),
        cols,
        img_even,
        img_odd,
        mass_even,
        mass_odd,
        known,
        kernel,
        turned,
        wide,
        alias={8: 0, 9: 1, 10: 2},
        scratch=lanes,
        flops=held * models * COST,
    )
    fixed = (cols_even, cols_odd, mass_even, mass_odd, kernel, turned, wide)
    for iteration in range(1, ITERS - 1):
        sums = call(iterate, shape(1, models), sums, swap(sums, 1), *fixed, scratch=lanes)
    both, row_scale = call(
        functools.partial(last, rows),
        (shape(models // LANES + FEAT, LANES), shape(1, rows)),
        sums,
        swap(sums, 1),
        *fixed,
        img_even,
        img_odd,
        scratch=lanes,
    )
    return call(
        finish,
        (shape(FEAT, rows), shape(FEAT, share)),
        both,
        swap(both, 1),
        cols_even,
        cols_odd,
        row_scale,
        mdl_even,
        mdl_odd,
        turned,
    )


def split(img_feat, mdl_feat, img_mass, mdl_mass):
    factor = inv_temp / FEAT
    share = mdl_feat.shape[1]
    img_unit = normalize(img_feat)
    mdl_unit = lax.all_gather(normalize(mdl_feat), "img", axis=1, tiled=True)
    scores = lax.dot_general(
        img_unit, mdl_unit, (((0,), (0,)), ((), ())), preferred_element_type=F32
    )
    kernel = jnp.exp(scores * factor).astype(BF16)
    col_low = jnp.ones((mdl_unit.shape[1],), BF16)
    for iteration in range(ITERS):
        row_scale = img_mass / jnp.dot(kernel, col_low, preferred_element_type=F32)
        sums = jnp.dot(row_scale.astype(BF16), kernel, preferred_element_type=F32)
        col_scale = mdl_mass / lax.psum(sums, "img")
        col_low = col_scale.astype(BF16)
    weighted = (mdl_unit.astype(F32) * col_scale[None, :]).astype(BF16)
    grad_img = lax.dot_general(
        weighted, kernel, (((1,), (1,)), ((), ())), preferred_element_type=F32
    )
    grad_img = -(grad_img * row_scale[None, :])
    row_feat = (img_unit.astype(F32) * row_scale[None, :]).astype(BF16)
    terms = lax.dot_general(
        kernel, row_feat, (((0,), (1,)), ((), ())), preferred_element_type=F32
    )
    summed = lax.psum_scatter(terms, "img", scatter_dimension=0, tiled=True)
    offset = lax.axis_index("img") * share
    own_scale = lax.dynamic_slice_in_dim(col_scale, offset, share, 0)
    grad_mdl = -(summed * own_scale[:, None]).T
    return (grad_img, grad_mdl)


def shards(count, img_feat, mdl_feat, img_mass, mdl_mass):
    groups = count // 2
    rows, share = img_feat.shape[1], mdl_feat.shape[1]
    resident = (2 + 2 + 4 // 2) * (groups * rows) * (count * share)
    fits = (
        count == 2 * groups
        and groups >= 4
        and groups & (groups - 1) == 0
        and 2 * share == LANES
        and rows % LANES == 0
        and 3 * (rows // LANES) <= FEAT // 2
        and resident <= RESIDENT
    )
    if fits:
        return replicated(count, img_feat, mdl_feat, img_mass, mdl_mass)
    return split(img_feat, mdl_feat, img_mass, mdl_mass)


def solution(mesh):
    placed = (P(None, ("fish", "img")), P(None, ("fish", "img")), P(("fish", "img")), P("fish"))
    return jax.shard_map(
        functools.partial(shards, mesh.shape["img"]),
        mesh=mesh,
        in_specs=placed,
        out_specs=(P(None, ("fish", "img")), P(None, ("fish", "img"))),
        check_vma=False,
    )
```
